1024 devices in a mesh: cluster: 64 (over y, x, core), split: 16 (over z).
Axes of the slice: x: 4, y: 8, z: 16, core: 2. Of those that a mesh axis runs over, the one named last changes fastest.
Arguments:
- embeddings: bfloat16 [131072, 1024], P(('cluster', 'split'))
- assignment: int32 [131072], P(('cluster', 'split')), may hold values from 0 to 63, as said below
Outputs:
- nearest_cosine: float32 [64, 16, 256], P('cluster', 'split')
- centroid_distance: float32 [64, 16, 256], P('cluster', 'split')
The draws below stay inside these ranges and needn't reach their ends.
Inputs may be any that keep to these rules, and one draw needn't show every extreme that they name: `assignment`: in each aligned block of 128 rows exactly 32 clusters appear, each on exactly 4 rows; every cluster appears in some block. `embeddings`: no row is all zero.
All inputs are finite; a program needn't handle non-finite values.
Results may differ from the reference program's by a relative error of at most 0.00045.
Values may be sent and summed in bfloat16 or wider, within the bound.
No kernel may reach another device: no remote copies, remote signals or barrier semaphores. Data moves between devices by JAX's collectives and lax.ppermute only.
A program may use at most 32 MiB of HBM per device.

```python
import jax
import jax.numpy as jnp
from jax import lax

D = 1024
ROWS_DEV = 128
CLUSTERS = 64
BLOCKS = 1024
ROWS = 131072
GROUPS = 32
CAP = 4
SLOTS = 256
N_SPLIT = 16


def cluster_draw(key):
    base_key = jax.random.fold_in(key, 11)
    heat = jax.random.randint(jax.random.fold_in(base_key, 1), (CLUSTERS,), 0, 3) * 24576
    jitter = jax.random.randint(jax.random.fold_in(base_key, 2), (BLOCKS, CLUSTERS), 0, 65536)
    block_ids = jnp.arange(BLOCKS, dtype=jnp.int32)
    cluster_ids = jnp.arange(CLUSTERS, dtype=jnp.int32)
    forced = (cluster_ids[None, :] == (block_ids % CLUSTERS)[:, None]).astype(jnp.int32) * 4194304
    scores = (jitter + heat[None, :] + forced) * CLUSTERS + cluster_ids[None, :]
    chosen = lax.top_k(scores, GROUPS)[1].astype(jnp.int32)
    repeated = jnp.repeat(chosen, CAP, axis=1)
    order_keys = jax.random.randint(jax.random.fold_in(base_key, 3), (BLOCKS, ROWS_DEV), 0, 65536) * ROWS_DEV + jnp.arange(ROWS_DEV, dtype=jnp.int32)[None, :]
    order = jnp.argsort(order_keys, axis=1, stable=True)
    shuffled = jnp.take_along_axis(repeated, order, axis=1)
    return shuffled.reshape(ROWS).astype(jnp.int32)


def draw_assignment(key, part):
    return cluster_draw(key)


def draw_embeddings(key, part):
    clusters_of_rows = cluster_draw(key)
    emb_key = jax.random.fold_in(key, 23)
    protos = jax.random.normal(jax.random.fold_in(emb_key, 1), (CLUSTERS, D), jnp.float32)
    shared_count = max(ROWS // CLUSTERS // 2, 1)
    shared_id = jax.random.randint(jax.random.fold_in(emb_key, 2), (ROWS,), 0, shared_count)
    shared_code = clusters_of_rows * shared_count + shared_id
    shared_key = jax.random.fold_in(emb_key, 3)

    def shared_vector(code_value):
        return jax.random.normal(jax.random.fold_in(shared_key, code_value), (D,), jnp.float32)
    shared_part = jax.vmap(shared_vector)(shared_code)
    private_part = 0.5 * jax.random.normal(jax.random.fold_in(emb_key, 4), (ROWS, D), jnp.float32)
    return (0.25 * protos[clusters_of_rows] + shared_part + private_part).astype(jnp.bfloat16)


def setup_inputs(seed: int = 0) -> dict:
    key_of = jax.random.split(jax.random.key(seed), 3)
    return {
        "embeddings": draw_embeddings(jax.random.fold_in(key_of[2], 71), 0),
        "assignment": draw_assignment(jax.random.fold_in(key_of[2], 71), 0),
    }


epsilon = 1e-06

def normalize_rows(values):
    as_float = values.astype(jnp.float32)
    return (as_float * lax.rsqrt(lax.optimization_barrier(jnp.sum(as_float * as_float, axis=1, keepdims=True)) + epsilon)).astype(jnp.bfloat16)

def per_cluster(inputs):
    members, alive_mask = inputs
    member_f32 = members.astype(jnp.float32)
    center = lax.optimization_barrier(jnp.sum(member_f32 * alive_mask[:, None], axis=0))
    centre_cos = lax.optimization_barrier(jnp.sum(member_f32 * center[None, :], axis=1)) * lax.rsqrt(jnp.sum(center * center) + epsilon)
    distance = jnp.where(alive_mask > 0, 1.0 - centre_cos, 0.0)
    scores = jnp.dot(members, members.T, preferred_element_type=jnp.float32)
    positions = jnp.arange(members.shape[0], dtype=jnp.int32)
    usable = (alive_mask[None, :] > 0) & (positions[None, :] != positions[:, None])
    nearest = lax.optimization_barrier(jnp.max(jnp.where(usable, scores, -2.0), axis=1))
    nearest = jnp.where(alive_mask > 0, nearest, 0.0)
    return (nearest, distance)

def reference(embeddings, assignment):
    normed = normalize_rows(embeddings)
    block_of_row = jnp.arange(ROWS, dtype=jnp.int32) // ROWS_DEV
    owner_index = block_of_row // N_SPLIT
    split_index = block_of_row % N_SPLIT
    onehot = (assignment.reshape(BLOCKS, ROWS_DEV)[:, :, None] == jnp.arange(CLUSTERS, dtype=jnp.int32)[None, None, :]).astype(jnp.int32)
    rank_in_owner = lax.optimization_barrier(jnp.sum((jnp.cumsum(onehot, axis=1) - 1) * onehot, axis=2)).reshape(ROWS).astype(jnp.int32)
    target = ((assignment * N_SPLIT + split_index) * SLOTS + owner_index * CAP + rank_in_owner).astype(jnp.int32)
    placed = jnp.zeros((CLUSTERS * N_SPLIT * SLOTS, D), jnp.bfloat16).at[target].set(normed)
    alive_all = jnp.zeros((CLUSTERS * N_SPLIT * SLOTS,), jnp.float32).at[target].set(1.0)
    placed = placed.reshape(CLUSTERS, N_SPLIT * SLOTS, D)
    alive_all = alive_all.reshape(CLUSTERS, N_SPLIT * SLOTS)
    nearest, distance = lax.map(per_cluster, (placed, alive_all))
    return (nearest.reshape(CLUSTERS, N_SPLIT, SLOTS), distance.reshape(CLUSTERS, N_SPLIT, SLOTS))
```

```python
import jax
import jax.numpy as jnp
from jax import lax
from jax.sharding import PartitionSpec as P

EPSILON = 1e-06
NEVER = -2.0
DEAD_MARK = 2.0
CHUNKS = 1


def normalize_rows(values):
    as_float = values.astype(jnp.float32)
    return (
        as_float * lax.rsqrt(jnp.sum(as_float * as_float, axis=1, keepdims=True) + EPSILON)
    ).astype(jnp.bfloat16)


def outgoing_rows(embeddings, assignment, owners, per_owner):
    row_count = embeddings.shape[0]
    slot_count = owners * per_owner
    normed = normalize_rows(embeddings)
    same = assignment[:, None] == assignment[None, :]
    earlier = jnp.arange(row_count)[None, :] < jnp.arange(row_count)[:, None]
    rank = jnp.sum((same & earlier).astype(jnp.int32), axis=1)
    target = assignment * per_owner + rank
    table = target[None, :] == jnp.arange(slot_count, dtype=jnp.int32)[:, None]
    rows = jnp.dot(table.astype(jnp.bfloat16), normed, preferred_element_type=jnp.float32)
    filled = jnp.any(table, axis=1)
    first = jnp.arange(embeddings.shape[1], dtype=jnp.int32)[None, :] == 0
    rows = jnp.where(first & ~filled[:, None], DEAD_MARK, rows)
    return rows.astype(jnp.bfloat16)


def alive_of(block):
    return block[:, 0] < jnp.bfloat16(1.5)


def dots(a, b):
    return lax.dot_general(a, b, (((1,), (1,)), ((), ())), preferred_element_type=jnp.float32)


def row_best(a, b, b_alive):
    return jnp.max(jnp.where(b_alive[None, :], dots(a, b), NEVER), axis=1)


def shift(value, by, n):
    return lax.ppermute(value, "split", [(i, (i + by) % n) for i in range(n)])


def local(embeddings, assignment):
    owners = lax.axis_size("cluster")
    n = lax.axis_size("split")
    width = embeddings.shape[1]
    per_owner = 2 * embeddings.shape[0] // owners
    slots = owners * per_owner
    send = outgoing_rows(embeddings, assignment, owners, per_owner)
    own = lax.all_to_all(
        send.reshape(owners, per_owner, width), "cluster", split_axis=0, concat_axis=0, tiled=True
    ).reshape(slots, width)

    size = slots // CHUNKS
    down = [[own[c * size : (c + 1) * size]] for c in range(CHUNKS)]
    up = [[own[c * size : (c + 1) * size]] for c in range(CHUNKS)]
    for step in range(4):
        for c in range(CHUNKS):
            down[c].append(shift(down[c][-1], 1, n))
            up[c].append(shift(up[c][-1], -1, n))
    block = {0: [own]}
    for d in range(1, 5):
        block[-d] = [down[c][d] for c in range(CHUNKS)]
        block[d] = [up[c][d] for c in range(CHUNKS)]
    alive = {d: [alive_of(x) for x in block[d]] for d in block}

    diagonal = jnp.arange(slots)[None, :] == jnp.arange(slots)[:, None]
    own_alive = alive[0][0]
    best = jnp.max(jnp.where(own_alive[None, :] & ~diagonal, dots(own, own), NEVER), axis=1)
    for d in (-1, 1, -2, 2, -3, 3, -4, 4):
        for x, live in zip(block[d], alive[d]):
            best = jnp.maximum(best, row_best(own, x, live))

    def pair_best(p, q):
        return jnp.concatenate(
            [
                jnp.max(jnp.stack([row_best(a, b, l) for b, l in zip(block[q], alive[q])]), axis=0)
                for a in block[p]
            ]
        )

    r = {}

    def add(p, value):
        r[p] = value if p not in r else jnp.maximum(r[p], value)

    for p, q in ((-3, 2), (-3, 3)):
        add(p, pair_best(p, q))
        add(q, pair_best(q, p))
    early = {p: shift(v, p, n) for p, v in r.items()}
    r = {}
    add(-3, pair_best(-3, 4))
    add(4, pair_best(4, -3))
    add(4, pair_best(4, -4))
    late = {p: shift(v, p, n) for p, v in r.items()}
    for v in list(early.values()) + list(late.values()):
        best = jnp.maximum(best, v)
    nearest = jnp.where(own_alive, best, 0.0)

    total = 0.0
    for d in (-2, -1, 0, 1):
        for x, live in zip(block[d], alive[d]):
            total = total + jnp.dot(
                live.astype(jnp.bfloat16)[None, :], x, preferred_element_type=jnp.float32
            )
    total = total + shift(total, 4, n)
    total = total + shift(total, 8, n)
    center = total[0]
    cosine = jnp.sum(own.astype(jnp.float32) * center[None, :], axis=1) * lax.rsqrt(
        jnp.sum(center * center) + EPSILON
    )
    distance = jnp.where(own_alive, 1.0 - cosine, 0.0)
    return nearest.reshape(1, 1, slots), distance.reshape(1, 1, slots)


def solution(mesh):
    in_specs = (P(("cluster", "split"), None), P(("cluster", "split")))
    out_specs = (P("cluster", "split", None), P("cluster", "split", None))
    return jax.shard_map(local, mesh=mesh, in_specs=in_specs, out_specs=out_specs, check_vma=False)
```

```python
import jax
import jax.numpy as jnp
from jax import lax
from jax.sharding import PartitionSpec as P

EPSILON = 1e-06
NEVER = -2.0
DEAD_MARK = 2.0
CHUNKS = 2


def normalize_rows(values):
    as_float = values.astype(jnp.float32)
    return (
        as_float * lax.rsqrt(jnp.sum(as_float * as_float, axis=1, keepdims=True) + EPSILON)
    ).astype(jnp.bfloat16)


def outgoing_rows(embeddings, assignment, owners, per_owner):
    row_count = embeddings.shape[0]
    slot_count = owners * per_owner
    normed = normalize_rows(embeddings)
    same = assignment[:, None] == assignment[None, :]
    earlier = jnp.arange(row_count)[None, :] < jnp.arange(row_count)[:, None]
    rank = jnp.sum((same & earlier).astype(jnp.int32), axis=1)
    target = assignment * per_owner + rank
    table = target[None, :] == jnp.arange(slot_count, dtype=jnp.int32)[:, None]
    rows = jnp.dot(table.astype(jnp.bfloat16), normed, preferred_element_type=jnp.float32)
    filled = jnp.any(table, axis=1)
    first = jnp.arange(embeddings.shape[1], dtype=jnp.int32)[None, :] == 0
    rows = jnp.where(first & ~filled[:, None], DEAD_MARK, rows)
    return rows.astype(jnp.bfloat16)


def dots(a, b):
    return sum(
        lax.dot_general(x, y, (((1,), (1,)), ((), ())), preferred_element_type=jnp.float32)
        for x, y in zip(a, b)
    )


def best_over(far, rows):
    alive = far[0][:, 0:1] < 1.5
    return jnp.max(jnp.where(alive, dots(far, rows), NEVER), axis=0)


def shift(value, by, n):
    return lax.ppermute(value, "split", [(i, (i + by) % n) for i in range(n)])


def local(embeddings, assignment):
    owners = lax.axis_size("cluster")
    n = lax.axis_size("split")
    width = embeddings.shape[1]
    per_owner = 2 * embeddings.shape[0] // owners
    slots = owners * per_owner
    send = outgoing_rows(embeddings, assignment, owners, per_owner)
    part = width // CHUNKS
    own = [
        lax.all_to_all(
            send[:, c * part : (c + 1) * part].reshape(owners, per_owner, part),
            "cluster",
            split_axis=0,
            concat_axis=0,
            tiled=True,
        ).reshape(slots, part)
        for c in range(CHUNKS)
    ]

    block = {0: own}
    for step in range(1, 5):
        block[-step] = [shift(x, 1, n) for x in block[1 - step]]
        block[step] = [shift(x, -1, n) for x in block[step - 1]]

    alive = own[0][:, 0] < 1.5
    index = jnp.arange(slots)
    usable = alive[:, None] & (index[None, :] != index[:, None])
    best = jnp.max(jnp.where(usable, dots(own, own), NEVER), axis=0)
    for d in (-1, 1, -2, 2, -3, 3, -4, 4):
        best = jnp.maximum(best, best_over(block[d], own))

    message = {
        -4: best_over(block[2], block[-4]),
        -3: jnp.maximum(best_over(block[2], block[-3]), best_over(block[4], block[-3])),
        2: jnp.maximum(best_over(block[-3], block[2]), best_over(block[-4], block[2])),
        4: jnp.maximum(best_over(block[-3], block[4]), best_over(block[-4], block[4])),
    }

    sums = []
    for c in range(CHUNKS):
        total = 0.0
        for d in range(-4, 4):
            weight = (block[d][0][:, 0:1] < 1.5).astype(jnp.bfloat16)
            total = total + lax.dot_general(
                weight, block[d][c], (((0,), (0,)), ((), ())), preferred_element_type=jnp.float32
            )
        sums.append(total[0])
    for d in (-4, 4):
        message[d] = jnp.concatenate([message[d]] + sums)
    arrived = {d: shift(v, d, n) for d, v in message.items()}
    for v in arrived.values():
        best = jnp.maximum(best, v[:slots])
    nearest = jnp.where(alive, best, 0.0)

    center = arrived[-4][slots:] + arrived[4][slots:]
    cosine = sum(
        jnp.sum(x.astype(jnp.float32) * center[None, c * part : (c + 1) * part], axis=1)
        for c, x in enumerate(own)
    ) * lax.rsqrt(jnp.sum(center * center) + EPSILON)
    distance = jnp.where(alive, 1.0 - cosine, 0.0)
    return nearest.reshape(1, 1, slots), distance.reshape(1, 1, slots)


def solution(mesh):
    in_specs = (P(("cluster", "split"), None), P(("cluster", "split")))
    out_specs = (P("cluster", "split", None), P("cluster", "split", None))
    return jax.shard_map(local, mesh=mesh, in_specs=in_specs, out_specs=out_specs, check_vma=False)
```

```python
import jax
import jax.numpy as jnp
from jax import lax
from jax.sharding import PartitionSpec as P

EPSILON = 1e-06
NEVER = -2.0
DEAD_MARK = 2.0
REACH = (5, 3)


def normalize_rows(values):
    as_float = values.astype(jnp.float32)
    return (
        as_float * lax.rsqrt(jnp.sum(as_float * as_float, axis=1, keepdims=True) + EPSILON)
    ).astype(jnp.bfloat16)


def outgoing_rows(embeddings, assignment, owners, per_owner):
    row_count = embeddings.shape[0]
    slot_count = owners * per_owner
    normed = normalize_rows(embeddings)
    same = assignment[:, None] == assignment[None, :]
    earlier = jnp.arange(row_count)[None, :] < jnp.arange(row_count)[:, None]
    rank = jnp.sum((same & earlier).astype(jnp.int32), axis=1)
    target = assignment * per_owner + rank
    table = target[None, :] == jnp.arange(slot_count, dtype=jnp.int32)[:, None]
    rows = jnp.dot(table.astype(jnp.bfloat16), normed, preferred_element_type=jnp.float32)
    filled = jnp.any(table, axis=1)
    first = jnp.arange(embeddings.shape[1], dtype=jnp.int32)[None, :] == 0
    rows = jnp.where(first & ~filled[:, None], DEAD_MARK, rows)
    return rows.astype(jnp.bfloat16)


def dots(a, b):
    return lax.dot_general(a, b, (((1,), (1,)), ((), ())), preferred_element_type=jnp.float32)


def alive_column(block):
    return block[:, 0:1] < 1.5


def best_over(far, rows):
    return jnp.max(jnp.where(alive_column(far), dots(far, rows), NEVER), axis=0)


def member_sum(block):
    weight = alive_column(block).astype(jnp.bfloat16)
    return lax.dot_general(
        weight, block, (((0,), (0,)), ((), ())), preferred_element_type=jnp.float32
    )[0]


def along_ring(value, by, owners, n):
    pairs = [
        (c * n + s, c * n + (s + (by if c % 2 == 0 else -by)) % n)
        for c in range(owners)
        for s in range(n)
    ]
    return lax.ppermute(value, ("cluster", "split"), pairs)


def to_partner(value, owners):
    return lax.ppermute(value, "cluster", [(c, c ^ 1) for c in range(owners)])


def local(embeddings, assignment):
    owners = lax.axis_size("cluster")
    n = lax.axis_size("split")
    width = embeddings.shape[1]
    per_owner = 2 * embeddings.shape[0] // owners
    slots = owners * per_owner
    send = outgoing_rows(embeddings, assignment, owners, per_owner)
    own = lax.all_to_all(
        send.reshape(owners, per_owner, width), "cluster", split_axis=0, concat_axis=0, tiled=True
    ).reshape(slots, width)

    mine = [own]
    other = [to_partner(own, owners)]
    for step in range(max(REACH)):
        if step < REACH[0]:
            mine.append(along_ring(mine[-1], 1, owners, n))
        if step < REACH[1]:
            other.append(along_ring(other[-1], 1, owners, n))
    ahead = {q: to_partner(other[q], owners) for q in (2, 3)}

    alive = own[:, 0] < 1.5
    index = jnp.arange(slots)
    usable = alive[:, None] & (index[None, :] != index[:, None])
    best = jnp.max(jnp.where(usable, dots(own, own), NEVER), axis=0)
    for p in range(1, 6):
        best = jnp.maximum(best, best_over(mine[p], own))
    for_partner = best_over(other[1], other[0])
    for q in (2, 3):
        for_partner = jnp.maximum(for_partner, best_over(other[q], other[0]))
    best = jnp.maximum(best, to_partner(for_partner, owners))

    to_four = jnp.maximum(best_over(own, mine[4]), best_over(ahead[2], mine[4]))
    to_two = jnp.maximum(best_over(mine[4], ahead[2]), best_over(mine[5], ahead[2]))

    behind = sum(member_sum(x) for x in mine)
    two = member_sum(ahead[2])
    four, ahead[3] = lax.optimization_barrier((jnp.concatenate([to_four, two]), ahead[3]))
    to_five = jnp.maximum(
        jnp.maximum(best_over(own, mine[5]), best_over(ahead[2], mine[5])),
        best_over(ahead[3], mine[5]),
    )
    messages = {
        -4: four,
        -5: jnp.concatenate([to_five, behind + two + member_sum(ahead[3])]),
        2: jnp.concatenate([to_two, behind]),
    }
    center = member_sum(mine[1])
    for by, message in messages.items():
        arrived = along_ring(message, by, owners, n)
        best = jnp.maximum(best, arrived[:slots])
        center = center + arrived[slots:]
    nearest = jnp.where(alive, best, 0.0)
    cosine = jnp.sum(own.astype(jnp.float32) * center[None, :], axis=1) * lax.rsqrt(
        jnp.sum(center * center) + EPSILON
    )
    distance = jnp.where(alive, 1.0 - cosine, 0.0)
    return nearest.reshape(1, 1, slots), distance.reshape(1, 1, slots)


def solution(mesh):
    in_specs = (P(("cluster", "split"), None), P(("cluster", "split")))
    out_specs = (P("cluster", "split", None), P("cluster", "split", None))
    return jax.shard_map(local, mesh=mesh, in_specs=in_specs, out_specs=out_specs, check_vma=False)
```

```python
import itertools

import jax
import jax.numpy as jnp
import numpy as np
from jax import lax
from jax.sharding import Mesh
from jax.sharding import PartitionSpec as P

EPSILON = 1e-06
NEVER = -2.0
DEAD_MARK = 2.0


def normalize_rows(values):
    as_float = values.astype(jnp.float32)
    return (
        as_float * lax.rsqrt(jnp.sum(as_float * as_float, axis=1, keepdims=True) + EPSILON)
    ).astype(jnp.bfloat16)


def outgoing_rows(embeddings, assignment, owners, per_owner):
    row_count = embeddings.shape[0]
    slot_count = owners * per_owner
    normed = normalize_rows(embeddings)
    same = assignment[:, None] == assignment[None, :]
    earlier = jnp.arange(row_count)[None, :] < jnp.arange(row_count)[:, None]
    rank = jnp.sum((same & earlier).astype(jnp.int32), axis=1)
    target = assignment * per_owner + rank
    table = target[None, :] == jnp.arange(slot_count, dtype=jnp.int32)[:, None]
    rows = jnp.dot(table.astype(jnp.bfloat16), normed, preferred_element_type=jnp.float32)
    filled = jnp.any(table, axis=1)
    first = jnp.arange(embeddings.shape[1], dtype=jnp.int32)[None, :] == 0
    rows = jnp.where(first & ~filled[:, None], DEAD_MARK, rows)
    return rows.astype(jnp.bfloat16)


DEAD_BEST = -8.0
ROWS = 16
HOME = (2, 4, 2)
HELD = ((0, 0, 0), (0, 0, 1), (0, 1, 0), (0, 3, 0), (1, 1, 0), (1, 3, 1))


def plus(a, b):
    return tuple((x + y) % d for x, y, d in zip(a, b, HOME))


def number(place):
    return (place[0] * HOME[1] + place[1]) * HOME[2] + place[2]


PLACES = list(itertools.product(*[range(d) for d in HOME]))


def choose_tiles():
    options = {}
    for p, q in itertools.permutations(HELD, 2):
        gap = plus(q, tuple(-x for x in p))
        options.setdefault(gap, []).append((p, q))
    for count in range(1, len(HELD) + 1):
        for rows in itertools.combinations(HELD, count):
            if rows[0] != HELD[0]:
                continue
            picks = [[t for t in options[gap] if t[0] in rows] for gap in sorted(options)]
            if len(picks) == len(PLACES) - 1 and all(picks):
                return rows, [t[0] for t in picks]
    raise ValueError("no cover")


TARGETS, TILES = choose_tiles()


def dots(a, b):
    return lax.dot_general(a, b, (((1,), (1,)), ((), ())), preferred_element_type=jnp.float32)


def best_and_sum(far, rows, diagonal):
    alive = far[:, 0:1] < 1.5
    scores = dots(far, rows)
    total = jnp.sum(jnp.where(alive, scores, 0.0), axis=0)
    if diagonal:
        index = jnp.arange(far.shape[0])
        alive = alive & (index[None, :] != index[:, None])
    return jnp.max(jnp.where(alive, scores, NEVER), axis=0), total


def exact_dot(a, b):
    return jnp.dot(a, b, precision=lax.Precision.HIGHEST, preferred_element_type=jnp.float32)


def local(embeddings, assignment):
    home = ("yl", "x", "core")
    far_y = lax.axis_size("yh")
    n = lax.axis_size("z")
    owners = far_y * len(PLACES)
    width = embeddings.shape[1]
    per_owner = 2 * embeddings.shape[0] // owners
    slots = owners * per_owner
    send = outgoing_rows(embeddings, assignment, owners, per_owner)
    own = lax.all_to_all(
        send.reshape(owners, per_owner, width),
        ("yh", "z"),
        split_axis=0,
        concat_axis=0,
        tiled=True,
    ).reshape(slots, width)
    block = {HELD[0]: own}
    for d in HELD[1:]:
        pairs = [(number(plus(u, d)), number(u)) for u in PLACES]
        block[d] = lax.ppermute(own, home, pairs)

    best, total = {}, {}
    best[HELD[0]], total[HELD[0]] = best_and_sum(own, own, True)
    for p, q in TILES:
        b, t = best_and_sum(block[q], block[p], False)
        best[p] = jnp.maximum(best[p], b) if p in best else b
        total[p] = total[p] + t if p in total else t
    square = 0.0
    for p in TARGETS:
        square = square + jnp.sum(jnp.where(block[p][:, 0] < 1.5, total[p], 0.0))
    best[HELD[0]] = jnp.where(own[:, 0] < 1.5, best[HELD[0]], DEAD_BEST)
    count = len(TARGETS)
    values = jnp.stack(
        [best[p] for p in TARGETS]
        + [total[p] for p in TARGETS]
        + [jnp.full((slots,), square)] * (ROWS - 2 * count)
    )

    lane = np.arange(slots)
    lane_z = (lane // per_owner) % n
    lane_c = (lane // (per_owner * n)) * per_owner + lane % per_owner
    cells = far_y * per_owner
    group = 128 // cells
    spread = jnp.asarray((lane_c[:, None] == np.arange(128)[None, :] % cells), jnp.float32)
    of_z = jnp.asarray(np.arange(n)[:, None] == lane_z[None, :])
    keep = jnp.asarray(np.arange(group)[:, None] == np.arange(128)[None, :] // cells)
    chosen = jnp.where(of_z[:, None, :], values[None], 0.0).reshape(n * ROWS, slots)
    message = jnp.sum(
        jnp.where(keep[None], exact_dot(chosen, spread).reshape(-1, group, 128), 0.0), axis=1
    )
    places = len(PLACES)
    message = lax.ppermute(
        message, home + ("z",), [(u * n + z, z * n + u) for u in range(places) for z in range(n)]
    )
    arrived = lax.all_to_all(
        message.reshape(n, ROWS // group, 128), "z", split_axis=0, concat_axis=0, tiled=True
    ).reshape(-1, 1, 128)

    rows = jnp.where(keep[None], arrived, 0.0).reshape(places * ROWS, 128)
    wide = exact_dot(rows, spread.T).reshape(places, ROWS, slots)
    moved = np.full((places, ROWS), -1)
    for v in range(2 * count):
        for u in PLACES:
            moved[number(u), v] = number(plus(u, TARGETS[v % count]))
    moved = jnp.asarray(moved)[:, :, None]
    lane_u = jnp.asarray((lane // per_owner) % places)[None, None, :]
    result = jnp.sum(jnp.where((moved == lane_u) | (moved < 0), wide, 0.0), axis=0)
    alive = result[0] > NEVER - 1.0
    nearest = jnp.where(alive, jnp.max(result[:count], axis=0), 0.0)
    cosine = jnp.sum(result[count : 2 * count], axis=0) * lax.rsqrt(result[2 * count] + EPSILON)
    distance = jnp.where(alive, 1.0 - cosine, 0.0)
    return nearest.reshape(1, 1, slots), distance.reshape(1, 1, slots)


def solution(mesh):
    names = ("yh", "yl", "x", "core", "z")
    n = mesh.shape["split"]
    parts = Mesh(mesh.devices.reshape(-1, *HOME, n), names)
    in_specs = (P(names, None), P(names))
    out_specs = (P(names[:4], "z", None), P(names[:4], "z", None))
    return jax.shard_map(local, mesh=parts, in_specs=in_specs, out_specs=out_specs, check_vma=False)
```

```python
import itertools

import jax
import jax.numpy as jnp
import numpy as np
from jax import lax
from jax.experimental import pallas as pl
from jax.experimental.pallas import tpu as pltpu
from jax.sharding import Mesh
from jax.sharding import PartitionSpec as P

EPSILON = 1e-06
NEVER = -2.0
DEAD_MARK = 2.0


def normalize_rows(values):
    as_float = values.astype(jnp.float32)
    return (
        as_float * lax.rsqrt(jnp.sum(as_float * as_float, axis=1, keepdims=True) + EPSILON)
    ).astype(jnp.bfloat16)


def outgoing_rows(embeddings, assignment, owners, per_owner):
    row_count = embeddings.shape[0]
    slot_count = owners * per_owner
    normed = normalize_rows(embeddings)
    same = assignment[:, None] == assignment[None, :]
    earlier = jnp.arange(row_count)[None, :] < jnp.arange(row_count)[:, None]
    rank = jnp.sum((same & earlier).astype(jnp.int32), axis=1)
    target = assignment * per_owner + rank
    table = target[None, :] == jnp.arange(slot_count, dtype=jnp.int32)[:, None]
    rows = jnp.dot(table.astype(jnp.bfloat16), normed, preferred_element_type=jnp.float32)
    filled = jnp.any(table, axis=1)
    first = jnp.arange(embeddings.shape[1], dtype=jnp.int32)[None, :] == 0
    rows = jnp.where(first & ~filled[:, None], DEAD_MARK, rows)
    return rows.astype(jnp.bfloat16)


DEAD_BEST = -8.0
ROWS = 16
HOME = (2, 4, 2)
OWN, C, Y, YC = (0, 0, 0), (0, 0, 1), (1, 0, 0), (1, 0, 1)
X1, X2 = (0, 1, 0), (0, 2, 0)
TARGETS = (OWN, C, Y, YC, X1)
COUNT = len(TARGETS)


def plus(a, b):
    return tuple((x + y) % d for x, y, d in zip(a, b, HOME))


def number(place):
    return (place[0] * HOME[1] + place[1]) * HOME[2] + place[2]


PLACES = list(itertools.product(*[range(d) for d in HOME]))


def from_place(value, d):
    pairs = [(number(plus(u, d)), number(u)) for u in PLACES]
    return lax.ppermute(value, ("yl", "x", "core"), pairs)


def dots(a, b):
    return lax.dot_general(a, b, (((1,), (1,)), ((), ())), preferred_element_type=jnp.float32)


def best_and_sum(far, rows, diagonal=False):
    alive = far[:, 0:1].astype(jnp.float32) < 1.5
    scores = dots(far, rows)
    total = jnp.sum(jnp.where(alive, scores, 0.0), axis=0, keepdims=True)
    if diagonal:
        same = lax.broadcasted_iota(jnp.int32, scores.shape, 0) == lax.broadcasted_iota(
            jnp.int32, scores.shape, 1
        )
        scores = jnp.where(same, NEVER, scores)
    return jnp.max(jnp.where(alive, scores, NEVER), axis=0, keepdims=True), total


def first_kernel(own, c, y, yc, x1, out):
    held = [own[...], c[...], y[...], yc[...], x1[...]]
    best, total = best_and_sum(held[0], held[0], True)
    best, total = [best], [total]
    pairs = [(0, 1), (0, 2), (0, 3), (0, 4), (1, 4), (2, 4), (3, 4), (4, 0), (4, 1), (4, 2), (4, 3)]
    for p, q in pairs:
        b, t = best_and_sum(held[q], held[p])
        if p < len(best):
            best[p], total[p] = jnp.maximum(best[p], b), total[p] + t
        else:
            best.append(b)
            total.append(t)
    first = (lax.broadcasted_iota(jnp.int32, (8, held[0].shape[1]), 1) == 0).astype(jnp.bfloat16)
    marks = [dots(first, x)[0:1] for x in held]
    out[...] = jnp.concatenate(best + total + marks + [marks[0]], axis=0)


def last_kernel(partial, own, c, y, yc, x2, spread, out):
    best = partial[0:COUNT, :]
    total = partial[COUNT : 2 * COUNT, :]
    alive = partial[2 * COUNT : 3 * COUNT, :] < 1.5
    far = x2[...]
    late = [best_and_sum(far, x[...]) for x in (own, c, y, yc)]
    best = jnp.concatenate(
        [jnp.maximum(best[i : i + 1], late[i][0]) for i in range(4)] + [best[4:5]], axis=0
    )
    total = jnp.concatenate([total[i : i + 1] + late[i][1] for i in range(4)] + [total[4:5]], axis=0)
    square = jnp.sum(jnp.where(alive, total, 0.0))
    best = jnp.concatenate([jnp.where(alive[0:1], best[0:1], DEAD_BEST), best[1:]], axis=0)
    slots = best.shape[1]
    values = jnp.concatenate(
        [best, total, jnp.full((ROWS - 2 * COUNT, slots), square, jnp.float32)], axis=0
    )
    n = out.shape[0] * 8 // ROWS
    lane_z = lax.broadcasted_iota(jnp.int32, (n, ROWS, slots), 2) // 4 % n
    of_z = lane_z == lax.broadcasted_iota(jnp.int32, (n, ROWS, slots), 0)
    chosen = jnp.where(of_z, values[None], 0.0).reshape(n * ROWS, slots)
    wide = jnp.dot(
        chosen,
        spread[...],
        precision=lax.Precision.HIGHEST,
        preferred_element_type=jnp.float32,
    ).reshape(n * ROWS // 8, 8, 128)
    cells = 128 // 8
    keep = lax.broadcasted_iota(jnp.int32, wide.shape, 2) // cells == lax.broadcasted_iota(
        jnp.int32, wide.shape, 1
    )
    out[...] = jnp.sum(jnp.where(keep, wide, 0.0), axis=1)


def local(embeddings, assignment):
    home = ("yl", "x", "core")
    far_y = lax.axis_size("yh")
    n = lax.axis_size("z")
    places = len(PLACES)
    owners = far_y * places
    width = embeddings.shape[1]
    per_owner = 2 * embeddings.shape[0] // owners
    slots = owners * per_owner
    send = outgoing_rows(embeddings, assignment, owners, per_owner)
    own = lax.all_to_all(
        send.reshape(owners, per_owner, width),
        ("yh", "z"),
        split_axis=0,
        concat_axis=0,
        tiled=True,
    ).reshape(slots, width)
    x1 = from_place(own, X1)
    y = from_place(own, Y)
    c = from_place(own, C)
    yc = from_place(y, C)
    x2 = from_place(x1, X1)

    lane = np.arange(slots)
    lane_c = (lane // (per_owner * n)) * per_owner + lane % per_owner
    group = 8
    cells = 128 // group
    spread = jnp.asarray((lane_c[:, None] == np.arange(128)[None, :] % cells), jnp.float32)
    partial = pl.pallas_call(
        first_kernel,
        out_shape=jax.ShapeDtypeStruct((ROWS, slots), jnp.float32),
        in_specs=[pl.BlockSpec(memory_space=pltpu.VMEM)] * 5,
        out_specs=pl.BlockSpec(memory_space=pltpu.VMEM),
        cost_estimate=pl.CostEstimate(
            flops=24 * slots * slots * width, bytes_accessed=5 * slots * width * 2, transcendentals=0
        ),
    )(own, c, y, yc, x1)
    message = pl.pallas_call(
        last_kernel,
        out_shape=jax.ShapeDtypeStruct((n * ROWS // group, 128), jnp.float32),
        in_specs=[pl.BlockSpec(memory_space=pltpu.VMEM)] * 7,
        out_specs=pl.BlockSpec(memory_space=pltpu.VMEM),
        cost_estimate=pl.CostEstimate(
            flops=8 * slots * slots * width, bytes_accessed=5 * slots * width * 2, transcendentals=0
        ),
    )(partial, own, c, y, yc, x2, spread)

    message = lax.all_to_all(
        message.reshape(n, ROWS // group, 128), "z", split_axis=0, concat_axis=0, tiled=True
    )
    arrived = lax.all_to_all(message, home, split_axis=0, concat_axis=0, tiled=True).reshape(
        -1, 1, 128
    )

    keep = jnp.asarray(np.arange(group)[:, None] == np.arange(128)[None, :] // cells)
    rows = jnp.where(keep[None], arrived, 0.0).reshape(places * ROWS, 128)
    wide = jnp.dot(
        rows, spread.T, precision=lax.Precision.HIGHEST, preferred_element_type=jnp.float32
    ).reshape(places, ROWS, slots)
    moved = np.full((places, ROWS), -1)
    for v in range(2 * COUNT):
        for u in PLACES:
            moved[number(u), v] = number(plus(u, TARGETS[v % COUNT]))
    moved = jnp.asarray(moved)[:, :, None]
    lane_u = jnp.asarray((lane // per_owner) % places)[None, None, :]
    result = jnp.sum(jnp.where((moved == lane_u) | (moved < 0), wide, 0.0), axis=0)
    alive = result[0] > NEVER - 1.0
    nearest = jnp.where(alive, jnp.max(result[:COUNT], axis=0), 0.0)
    cosine = jnp.sum(result[COUNT : 2 * COUNT], axis=0) * lax.rsqrt(result[2 * COUNT] + EPSILON)
    distance = jnp.where(alive, 1.0 - cosine, 0.0)
    return nearest.reshape(1, 1, slots), distance.reshape(1, 1, slots)


def solution(mesh):
    names = ("yh", "yl", "x", "core", "z")
    n = mesh.shape["split"]
    parts = Mesh(mesh.devices.reshape(-1, *HOME, n), names)
    in_specs = (P(names, None), P(names))
    out_specs = (P(names[:4], "z", None), P(names[:4], "z", None))
    return jax.shard_map(local, mesh=parts, in_specs=in_specs, out_specs=out_specs, check_vma=False)
```

```python
import itertools

import jax
import jax.numpy as jnp
from jax import lax
from jax.experimental import pallas as pl
from jax.experimental.pallas import tpu as pltpu
from jax.sharding import Mesh
from jax.sharding import PartitionSpec as P

EPSILON = 1e-06
NEVER = -2.0
DEAD_MARK = 2.0


def normalize_rows(values):
    as_float = values.astype(jnp.float32)
    return (
        as_float * lax.rsqrt(jnp.sum(as_float * as_float, axis=1, keepdims=True) + EPSILON)
    ).astype(jnp.bfloat16)


def outgoing_rows(embeddings, assignment, owners, per_owner):
    row_count = embeddings.shape[0]
    slot_count = owners * per_owner
    normed = normalize_rows(embeddings)
    same = assignment[:, None] == assignment[None, :]
    earlier = jnp.arange(row_count)[None, :] < jnp.arange(row_count)[:, None]
    rank = jnp.sum((same & earlier).astype(jnp.int32), axis=1)
    target = assignment * per_owner + rank
    table = target[None, :] == jnp.arange(slot_count, dtype=jnp.int32)[:, None]
    rows = jnp.dot(table.astype(jnp.bfloat16), normed, preferred_element_type=jnp.float32)
    filled = jnp.any(table, axis=1)
    first = jnp.arange(embeddings.shape[1], dtype=jnp.int32)[None, :] == 0
    rows = jnp.where(first & ~filled[:, None], DEAD_MARK, rows)
    return rows.astype(jnp.bfloat16)


DEAD_BEST = -8.0
ROWS = 16
HOME = (2, 4, 2)
OWN, C, Y, YC = (0, 0, 0), (0, 0, 1), (1, 0, 0), (1, 0, 1)
X1, X2 = (0, 1, 0), (0, 2, 0)
TARGETS = (OWN, C, Y, YC, X1)
COUNT = len(TARGETS)


def plus(a, b):
    return tuple((x + y) % d for x, y, d in zip(a, b, HOME))


def number(place):
    return (place[0] * HOME[1] + place[1]) * HOME[2] + place[2]


PLACES = list(itertools.product(*[range(d) for d in HOME]))


def from_place(value, d):
    pairs = [(number(plus(u, d)), number(u)) for u in PLACES]
    return lax.ppermute(value, ("yl", "x", "core"), pairs)


def dots(a, b):
    return lax.dot_general(a, b, (((1,), (1,)), ((), ())), preferred_element_type=jnp.float32)


def best_and_sum(far, rows, diagonal=False):
    alive = far[:, 0:1].astype(jnp.float32) < 1.5
    scores = dots(far, rows)
    total = jnp.sum(jnp.where(alive, scores, 0.0), axis=0, keepdims=True)
    if diagonal:
        same = lax.broadcasted_iota(jnp.int32, scores.shape, 0) == lax.broadcasted_iota(
            jnp.int32, scores.shape, 1
        )
        scores = jnp.where(same, NEVER, scores)
    return jnp.max(jnp.where(alive, scores, NEVER), axis=0, keepdims=True), total


def own_kernel(own, out):
    best, total = best_and_sum(own[...], own[...], True)
    out[...] = jnp.concatenate([best, total] * 4, axis=0)


def first_kernel(mine, own, y, swapped, x1, out):
    slots = own.shape[0]
    held = [own[...], swapped[:slots, :], y[...], swapped[slots:, :], x1[...]]
    best, total = [mine[0:1, :]], [mine[1:2, :]]
    pairs = [(0, 1), (0, 2), (0, 3), (0, 4), (1, 4), (2, 4), (3, 4), (4, 0), (4, 1), (4, 2), (4, 3)]
    for p, q in pairs:
        b, t = best_and_sum(held[q], held[p])
        if p < len(best):
            best[p], total[p] = jnp.maximum(best[p], b), total[p] + t
        else:
            best.append(b)
            total.append(t)
    first = (lax.broadcasted_iota(jnp.int32, (8, held[0].shape[1]), 1) == 0).astype(jnp.bfloat16)
    marks = [dots(first, x)[0:1] for x in held]
    out[...] = jnp.concatenate(best + total + marks + [marks[0]], axis=0)


def iota(shape, axis):
    return lax.broadcasted_iota(jnp.int32, shape, axis)


def exact_dot(a, b):
    return lax.dot_general(
        a,
        b,
        (((1,), (0,)), ((), ())),
        precision=lax.Precision.HIGHEST,
        preferred_element_type=jnp.float32,
    )


GROUP = 8
CELLS = 16


def cell_of(slot):
    return slot // 64 * 4 + slot % 4


def place_of(slot):
    return slot // 4 % 16


def last_kernel(partial, own, y, swapped, x2, out):
    best = partial[0:COUNT, :]
    total = partial[COUNT : 2 * COUNT, :]
    alive = partial[2 * COUNT : 3 * COUNT, :] < 1.5
    far = x2[...]
    slots = own.shape[0]
    targets = (own[...], swapped[:slots, :], y[...], swapped[slots:, :])
    late = [best_and_sum(far, x) for x in targets]
    best = jnp.concatenate(
        [jnp.maximum(best[i : i + 1], late[i][0]) for i in range(4)] + [best[4:5]], axis=0
    )
    total = jnp.concatenate([total[i : i + 1] + late[i][1] for i in range(4)] + [total[4:5]], axis=0)
    square = jnp.sum(jnp.where(alive, total, 0.0))
    best = jnp.concatenate([jnp.where(alive[0:1], best[0:1], DEAD_BEST), best[1:]], axis=0)
    values = jnp.concatenate(
        [best, total, jnp.full((ROWS - 2 * COUNT, slots), square, jnp.float32)], axis=0
    )
    n = out.shape[0] * GROUP // ROWS
    shape = (n, ROWS, slots)
    chosen = jnp.where(place_of(iota(shape, 2)) == iota(shape, 0), values[None], 0.0)
    shape = (slots, GROUP * CELLS)
    spread = (cell_of(iota(shape, 0)) == iota(shape, 1) % CELLS).astype(jnp.float32)
    wide = exact_dot(chosen.reshape(n * ROWS, slots), spread).reshape(-1, GROUP, GROUP * CELLS)
    keep = iota(wide.shape, 2) // CELLS == iota(wide.shape, 1)
    out[...] = jnp.sum(jnp.where(keep, wide, 0.0), axis=1)


def finish_kernel(arrived, nearest, distance):
    slots = nearest.shape[1]
    places = arrived.shape[0] * GROUP // ROWS
    shape = (arrived.shape[0], GROUP, GROUP * CELLS)
    keep = iota(shape, 2) // CELLS == iota(shape, 1)
    rows = jnp.where(keep, arrived[...][:, None, :], 0.0).reshape(places * ROWS, GROUP * CELLS)
    shape = (GROUP * CELLS, slots)
    spread = (cell_of(iota(shape, 1)) == iota(shape, 0) % CELLS).astype(jnp.float32)
    wide = exact_dot(rows, spread).reshape(places, ROWS, slots)
    u, v, to = (iota(wide.shape, axis) for axis in range(3))
    target = v % COUNT
    core = (u ^ jnp.where((target == 1) | (target == 3), 1, 0)) & 1
    low = (u ^ jnp.where((target == 2) | (target == 3), 8, 0)) & 8
    across = (u + jnp.where(target == 4, 2, 0)) & 6
    here = (core + low + across == place_of(to)) | (v >= 2 * COUNT)
    result = jnp.sum(jnp.where(here, wide, 0.0), axis=0)
    alive = result[0:1] > NEVER - 1.0
    best = jnp.max(result[0:COUNT], axis=0, keepdims=True)
    nearest[...] = jnp.where(alive, best, 0.0)
    cosine = jnp.sum(result[COUNT : 2 * COUNT], axis=0, keepdims=True) * lax.rsqrt(
        result[2 * COUNT : 2 * COUNT + 1] + EPSILON
    )
    distance[...] = jnp.where(alive, 1.0 - cosine, 0.0)


def on_chip(kernel, out_shape, flops, *operands):
    vmem = pl.BlockSpec(memory_space=pltpu.VMEM)
    single = isinstance(out_shape, jax.ShapeDtypeStruct)
    return pl.pallas_call(
        kernel,
        out_shape=out_shape,
        in_specs=[vmem] * len(operands),
        out_specs=vmem if single else [vmem] * len(out_shape),
        compiler_params=pltpu.CompilerParams(vmem_limit_bytes=16 * 2**20),
        cost_estimate=pl.CostEstimate(
            flops=flops, bytes_accessed=sum(x.size * 2 for x in operands), transcendentals=0
        ),
    )(*operands)


def local(embeddings, assignment):
    home = ("yl", "x", "core")
    far_y = lax.axis_size("yh")
    n = lax.axis_size("z")
    places = len(PLACES)
    owners = far_y * places
    width = embeddings.shape[1]
    per_owner = 2 * embeddings.shape[0] // owners
    slots = owners * per_owner
    send = outgoing_rows(embeddings, assignment, owners, per_owner)
    own = lax.all_to_all(
        send.reshape(owners, per_owner, width),
        ("yh", "z"),
        split_axis=0,
        concat_axis=0,
        tiled=True,
    ).reshape(slots, width)
    tile = 2 * slots * slots * width
    x1 = from_place(own, X1)
    mine = on_chip(own_kernel, jax.ShapeDtypeStruct((8, slots), jnp.float32), tile, own)
    y = from_place(own, Y)
    x2 = from_place(x1, X1)
    y, x1, mine = lax.optimization_barrier((y, x1, mine))
    swapped = from_place(jnp.concatenate([own, y]), C)
    partial = on_chip(
        first_kernel,
        jax.ShapeDtypeStruct((ROWS, slots), jnp.float32),
        0,
        mine,
        own,
        y,
        swapped,
        x1,
    )
    message = on_chip(
        last_kernel,
        jax.ShapeDtypeStruct((n * ROWS // GROUP, GROUP * CELLS), jnp.float32),
        4 * tile,
        partial,
        own,
        y,
        swapped,
        x2,
    )
    message = message.reshape(n, ROWS // GROUP, GROUP * CELLS)
    message = lax.all_to_all(message, "z", split_axis=0, concat_axis=0, tiled=True)
    message = lax.all_to_all(message, home, split_axis=0, concat_axis=0, tiled=True)
    row = jax.ShapeDtypeStruct((1, slots), jnp.float32)
    nearest, distance = on_chip(
        finish_kernel, (row, row), 0, message.reshape(places * ROWS // GROUP, GROUP * CELLS)
    )
    return nearest.reshape(1, 1, slots), distance.reshape(1, 1, slots)


def solution(mesh):
    names = ("yh", "yl", "x", "core", "z")
    n = mesh.shape["split"]
    parts = Mesh(mesh.devices.reshape(-1, *HOME, n), names)
    in_specs = (P(names, None), P(names))
    out_specs = (P(names[:4], "z", None), P(names[:4], "z", None))
    return jax.shard_map(local, mesh=parts, in_specs=in_specs, out_specs=out_specs, check_vma=False)
```

```python
import itertools

import jax
import jax.numpy as jnp
from jax import lax
from jax.experimental import pallas as pl
from jax.experimental.pallas import tpu as pltpu
from jax.sharding import Mesh
from jax.sharding import PartitionSpec as P

EPSILON = 1e-06
NEVER = -2.0
DEAD_MARK = 2.0


DEAD_BEST = -8.0
ROWS = 16
HOME = (2, 4, 2)
OWN, C, Y, YC = (0, 0, 0), (0, 0, 1), (1, 0, 0), (1, 0, 1)
X1, X2 = (0, 1, 0), (0, 2, 0)
TARGETS = (OWN, C, Y, YC, X1)
COUNT = len(TARGETS)


def plus(a, b):
    return tuple((x + y) % d for x, y, d in zip(a, b, HOME))


def number(place):
    return (place[0] * HOME[1] + place[1]) * HOME[2] + place[2]


PLACES = list(itertools.product(*[range(d) for d in HOME]))


def from_place(value, d):
    pairs = [(number(plus(u, d)), number(u)) for u in PLACES]
    return lax.ppermute(value, ("yl", "x", "core"), pairs)


def dots(a, b):
    return lax.dot_general(a, b, (((1,), (1,)), ((), ())), preferred_element_type=jnp.float32)


def best_and_sum(far, rows, diagonal=False):
    alive = far[:, 0:1].astype(jnp.float32) < 1.5
    scores = dots(far, rows)
    total = jnp.sum(jnp.where(alive, scores, 0.0), axis=0, keepdims=True)
    if diagonal:
        same = lax.broadcasted_iota(jnp.int32, scores.shape, 0) == lax.broadcasted_iota(
            jnp.int32, scores.shape, 1
        )
        scores = jnp.where(same, NEVER, scores)
    return jnp.max(jnp.where(alive, scores, NEVER), axis=0, keepdims=True), total


def send_kernel(embeddings, assignment, out):
    values = embeddings[...].astype(jnp.float32)
    scale = lax.rsqrt(jnp.sum(values * values, axis=1, keepdims=True) + EPSILON)
    normed = (values * scale).astype(jnp.bfloat16)
    rows, slots = values.shape[0], out.shape[0]
    along = jnp.broadcast_to(assignment[...].astype(jnp.float32), (rows, rows))
    earlier = iota((rows, rows), 0) < iota((rows, rows), 1)
    rank = jnp.sum(jnp.where((along == along.T) & earlier, 1.0, 0.0), axis=0, keepdims=True)
    slot = along[0:1] * (slots // 64) + rank
    table = (slot == iota((slots, rows), 0).astype(jnp.float32)).astype(jnp.float32)
    placed = jnp.dot(table.astype(jnp.bfloat16), normed, preferred_element_type=jnp.float32)
    empty = jnp.sum(table, axis=1, keepdims=True) < 0.5
    mark = empty & (iota(placed.shape, 1) == 0)
    out[...] = jnp.where(mark, DEAD_MARK, placed).astype(jnp.bfloat16)


def merge(old, new):
    return (jnp.maximum(old[0], new[0]), old[1] + new[1])


def near_kernel(own, y, x1, out):
    a, b, d = own[...], y[...], x1[...]
    stats = [
        merge(merge(best_and_sum(a, a, True), best_and_sum(b, a)), best_and_sum(d, a)),
        best_and_sum(d, b),
        merge(best_and_sum(a, d), best_and_sum(b, d)),
    ]
    out[...] = jnp.concatenate([b for b, _ in stats] + [t for _, t in stats] + [stats[0][0]] * 2)


def far_kernel(near, own, y, x2, out):
    far = x2[...]
    a, b = best_and_sum(far, own[...]), best_and_sum(far, y[...])
    best = jnp.maximum(near[0:2, :], jnp.concatenate([a[0], b[0]]))
    total = near[3:5, :] + jnp.concatenate([a[1], b[1]])
    out[...] = jnp.concatenate([best, near[2:3, :], total, near[5:8, :]])


def iota(shape, axis):
    return lax.broadcasted_iota(jnp.int32, shape, axis)


def exact_dot(a, b):
    return lax.dot_general(
        a,
        b,
        (((1,), (0,)), ((), ())),
        precision=lax.Precision.HIGHEST,
        preferred_element_type=jnp.float32,
    )


GROUP = 8
CELLS = 16


def cell_of(slot):
    return slot // 64 * 4 + slot % 4


def place_of(slot):
    return slot // 4 % 16


def last_kernel(seen, own, y, c, yc, x1, x2, out):
    held = [own[...], c[...], y[...], yc[...], x1[...]]
    far = x2[...]
    stats = [
        merge(best_and_sum(held[1], held[0]), best_and_sum(held[3], held[0])),
        merge(best_and_sum(held[4], held[1]), best_and_sum(far, held[1])),
        (seen[1:2, :], seen[4:5, :]),
        merge(best_and_sum(held[4], held[3]), best_and_sum(far, held[3])),
        merge(best_and_sum(held[1], held[4]), best_and_sum(held[3], held[4])),
    ]
    stats[0] = merge(stats[0], (seen[0:1, :], seen[3:4, :]))
    stats[4] = merge(stats[4], (seen[2:3, :], seen[5:6, :]))
    best = jnp.concatenate([b for b, _ in stats])
    total = jnp.concatenate([t for _, t in stats])
    slots = best.shape[1]
    first = (iota((8, own.shape[1]), 1) == 0).astype(jnp.bfloat16)
    alive = jnp.concatenate([dots(first, x)[0:1] for x in held]) < 1.5
    square = jnp.sum(jnp.where(alive, total, 0.0))
    best = jnp.concatenate([jnp.where(alive[0:1], best[0:1], DEAD_BEST), best[1:]], axis=0)
    values = jnp.concatenate(
        [best, total, jnp.full((ROWS - 2 * COUNT, slots), square, jnp.float32)], axis=0
    )
    n = out.shape[0] * GROUP // ROWS
    shape = (n, ROWS, slots)
    chosen = jnp.where(place_of(iota(shape, 2)) == iota(shape, 0), values[None], 0.0)
    shape = (slots, GROUP * CELLS)
    spread = (cell_of(iota(shape, 0)) == iota(shape, 1) % CELLS).astype(jnp.float32)
    wide = exact_dot(chosen.reshape(n * ROWS, slots), spread).reshape(-1, GROUP, GROUP * CELLS)
    keep = iota(wide.shape, 2) // CELLS == iota(wide.shape, 1)
    out[...] = jnp.sum(jnp.where(keep, wide, 0.0), axis=1)


def finish_kernel(arrived, nearest, distance):
    slots = nearest.shape[1]
    places = arrived.shape[0] * GROUP // ROWS
    shape = (arrived.shape[0], GROUP, GROUP * CELLS)
    keep = iota(shape, 2) // CELLS == iota(shape, 1)
    rows = jnp.where(keep, arrived[...][:, None, :], 0.0).reshape(places * ROWS, GROUP * CELLS)
    shape = (GROUP * CELLS, slots)
    spread = (cell_of(iota(shape, 1)) == iota(shape, 0) % CELLS).astype(jnp.float32)
    wide = exact_dot(rows, spread).reshape(places, ROWS, slots)
    u, v, to = (iota(wide.shape, axis) for axis in range(3))
    target = v % COUNT
    core = (u ^ jnp.where((target == 1) | (target == 3), 1, 0)) & 1
    low = (u ^ jnp.where((target == 2) | (target == 3), 8, 0)) & 8
    across = (u + jnp.where(target == 4, 2, 0)) & 6
    here = (core + low + across == place_of(to)) | (v >= 2 * COUNT)
    result = jnp.sum(jnp.where(here, wide, 0.0), axis=0)
    alive = result[0:1] > NEVER - 1.0
    best = jnp.max(result[0:COUNT], axis=0, keepdims=True)
    nearest[...] = jnp.where(alive, best, 0.0)
    cosine = jnp.sum(result[COUNT : 2 * COUNT], axis=0, keepdims=True) * lax.rsqrt(
        result[2 * COUNT : 2 * COUNT + 1] + EPSILON
    )
    distance[...] = jnp.where(alive, 1.0 - cosine, 0.0)


def on_chip(kernel, out_shape, flops, *operands):
    vmem = pl.BlockSpec(memory_space=pltpu.VMEM)
    single = isinstance(out_shape, jax.ShapeDtypeStruct)
    return pl.pallas_call(
        kernel,
        out_shape=out_shape,
        in_specs=[vmem] * len(operands),
        out_specs=vmem if single else [vmem] * len(out_shape),
        compiler_params=pltpu.CompilerParams(vmem_limit_bytes=16 * 2**20),
        cost_estimate=pl.CostEstimate(
            flops=flops, bytes_accessed=sum(x.size * 2 for x in operands), transcendentals=0
        ),
    )(*operands)


def local(embeddings, assignment):
    home = ("yl", "x", "core")
    far_y = lax.axis_size("yh")
    n = lax.axis_size("z")
    places = len(PLACES)
    owners = far_y * places
    width = embeddings.shape[1]
    per_owner = 2 * embeddings.shape[0] // owners
    slots = owners * per_owner
    rows = embeddings.shape[0]
    send = on_chip(
        send_kernel,
        jax.ShapeDtypeStruct((slots, width), jnp.bfloat16),
        2 * slots * rows * width,
        embeddings,
        assignment.reshape(1, rows),
    )
    own = lax.all_to_all(
        send.reshape(owners, per_owner, width),
        ("yh", "z"),
        split_axis=0,
        concat_axis=0,
        tiled=True,
    ).reshape(slots, width)
    tile = 2 * slots * slots * width
    x1 = from_place(own, X1)
    y = from_place(own, Y)
    x2 = from_place(x1, X1)
    stats = jax.ShapeDtypeStruct((8, slots), jnp.float32)
    near = on_chip(near_kernel, stats, 6 * tile, own, y, x1)
    first, later, near = lax.optimization_barrier((own, y, near))
    c = from_place(first, C)
    yc = from_place(later, C)
    seen = on_chip(far_kernel, stats, 2 * tile, near, own, y, x2)
    message = on_chip(
        last_kernel,
        jax.ShapeDtypeStruct((n * ROWS // GROUP, GROUP * CELLS), jnp.float32),
        8 * tile,
        seen,
        own,
        y,
        c,
        yc,
        x1,
        x2,
    )
    message = message.reshape(n, ROWS // GROUP, GROUP * CELLS)
    message = lax.all_to_all(message, "z", split_axis=0, concat_axis=0, tiled=True)
    message = lax.all_to_all(message, home, split_axis=0, concat_axis=0, tiled=True)
    row = jax.ShapeDtypeStruct((1, slots), jnp.float32)
    nearest, distance = on_chip(
        finish_kernel, (row, row), 0, message.reshape(places * ROWS // GROUP, GROUP * CELLS)
    )
    return nearest.reshape(1, 1, slots), distance.reshape(1, 1, slots)


def solution(mesh):
    names = ("yh", "yl", "x", "core", "z")
    n = mesh.shape["split"]
    parts = Mesh(mesh.devices.reshape(-1, *HOME, n), names)
    in_specs = (P(names, None), P(names))
    out_specs = (P(names[:4], "z", None), P(names[:4], "z", None))
    return jax.shard_map(local, mesh=parts, in_specs=in_specs, out_specs=out_specs, check_vma=False)
```

```python
import itertools

import jax
import jax.numpy as jnp
from jax import lax
from jax.experimental import pallas as pl
from jax.experimental.pallas import tpu as pltpu
from jax.sharding import Mesh
from jax.sharding import PartitionSpec as P

EPSILON = 1e-06
NEVER = -2.0
DEAD_MARK = 2.0


DEAD_BEST = -8.0
ROWS = 16
HOME = (2, 4, 2)
OWN, C, Y, YC = (0, 0, 0), (0, 0, 1), (1, 0, 0), (1, 0, 1)
X1, X2 = (0, 1, 0), (0, 2, 0)
TARGETS = (OWN, C, Y, YC, X1)
COUNT = len(TARGETS)


def plus(a, b):
    return tuple((x + y) % d for x, y, d in zip(a, b, HOME))


def number(place):
    return (place[0] * HOME[1] + place[1]) * HOME[2] + place[2]


PLACES = list(itertools.product(*[range(d) for d in HOME]))


def from_place(value, d):
    pairs = [(number(plus(u, d)), number(u)) for u in PLACES]
    return lax.ppermute(value, ("yl", "x", "core"), pairs)


def dots(a, b):
    return lax.dot_general(a, b, (((1,), (1,)), ((), ())), preferred_element_type=jnp.float32)


def best_and_sum(far, rows, diagonal=False):
    alive = far[:, 0:1].astype(jnp.float32) < 1.5
    scores = dots(far, rows)
    total = jnp.sum(jnp.where(alive, scores, 0.0), axis=0, keepdims=True)
    if diagonal:
        same = lax.broadcasted_iota(jnp.int32, scores.shape, 0) == lax.broadcasted_iota(
            jnp.int32, scores.shape, 1
        )
        scores = jnp.where(same, NEVER, scores)
    return jnp.max(jnp.where(alive, scores, NEVER), axis=0, keepdims=True), total


def send_kernel(embeddings, assignment, out):
    values = embeddings[...].astype(jnp.float32)
    scale = lax.rsqrt(jnp.sum(values * values, axis=1, keepdims=True) + EPSILON)
    normed = (values * scale).astype(jnp.bfloat16)
    rows, slots = values.shape[0], out.shape[0]
    along = jnp.broadcast_to(assignment[...].astype(jnp.float32), (rows, rows))
    earlier = iota((rows, rows), 0) < iota((rows, rows), 1)
    rank = jnp.sum(jnp.where((along == along.T) & earlier, 1.0, 0.0), axis=0, keepdims=True)
    slot = along[0:1] * (slots // 64) + rank
    table = (slot == iota((slots, rows), 0).astype(jnp.float32)).astype(jnp.float32)
    placed = jnp.dot(table.astype(jnp.bfloat16), normed, preferred_element_type=jnp.float32)
    empty = jnp.sum(table, axis=1, keepdims=True) < 0.5
    mark = empty & (iota(placed.shape, 1) == 0)
    out[...] = jnp.where(mark, DEAD_MARK, placed).astype(jnp.bfloat16)


def merge(old, new):
    return (jnp.maximum(old[0], new[0]), old[1] + new[1])


def near_kernel(own, y, x1, out):
    a, b, d = own[...], y[...], x1[...]
    stats = [
        merge(merge(best_and_sum(a, a, True), best_and_sum(b, a)), best_and_sum(d, a)),
        best_and_sum(d, b),
        merge(best_and_sum(a, d), best_and_sum(b, d)),
    ]
    out[...] = jnp.concatenate([b for b, _ in stats] + [t for _, t in stats] + [stats[0][0]] * 2)


def far_kernel(near, own, y, x2, out):
    far = x2[...]
    a, b = best_and_sum(far, own[...]), best_and_sum(far, y[...])
    best = jnp.maximum(near[0:2, :], jnp.concatenate([a[0], b[0]]))
    total = near[3:5, :] + jnp.concatenate([a[1], b[1]])
    out[...] = jnp.concatenate([best, near[2:3, :], total, near[5:8, :]])


def iota(shape, axis):
    return lax.broadcasted_iota(jnp.int32, shape, axis)


def exact_dot(a, b):
    return lax.dot_general(
        a,
        b,
        (((1,), (0,)), ((), ())),
        precision=lax.Precision.HIGHEST,
        preferred_element_type=jnp.float32,
    )


GROUP = 8
CELLS = 16


def cell_of(slot):
    return slot // 64 * 4 + slot % 4


def place_of(slot):
    return slot // 4 % 16


def last_kernel(seen, own, y, c, yc, x1, x2, out):
    held = [own[...], c[...], y[...], yc[...], x1[...]]
    far = x2[...]
    stats = [
        merge(best_and_sum(held[1], held[0]), best_and_sum(held[3], held[0])),
        merge(best_and_sum(held[4], held[1]), best_and_sum(far, held[1])),
        (seen[1:2, :], seen[4:5, :]),
        merge(best_and_sum(held[4], held[3]), best_and_sum(far, held[3])),
        merge(best_and_sum(held[1], held[4]), best_and_sum(held[3], held[4])),
    ]
    stats[0] = merge(stats[0], (seen[0:1, :], seen[3:4, :]))
    stats[4] = merge(stats[4], (seen[2:3, :], seen[5:6, :]))
    best = jnp.concatenate([b for b, _ in stats])
    total = jnp.concatenate([t for _, t in stats])
    slots = best.shape[1]
    first = (iota((8, own.shape[1]), 1) == 0).astype(jnp.bfloat16)
    alive = jnp.concatenate([dots(first, x)[0:1] for x in held]) < 1.5
    square = jnp.sum(jnp.where(alive, total, 0.0))
    best = jnp.concatenate([jnp.where(alive[0:1], best[0:1], DEAD_BEST), best[1:]], axis=0)
    values = jnp.concatenate(
        [best, total, jnp.full((ROWS - 2 * COUNT, slots), square, jnp.float32)], axis=0
    )
    n = out.shape[0] * GROUP // ROWS
    shape = (n, ROWS, slots)
    chosen = jnp.where(place_of(iota(shape, 2)) == iota(shape, 0), values[None], 0.0)
    shape = (slots, GROUP * CELLS)
    spread = (cell_of(iota(shape, 0)) == iota(shape, 1) % CELLS).astype(jnp.float32)
    wide = exact_dot(chosen.reshape(n * ROWS, slots), spread).reshape(-1, GROUP, GROUP * CELLS)
    keep = iota(wide.shape, 2) // CELLS == iota(wide.shape, 1)
    out[...] = jnp.sum(jnp.where(keep, wide, 0.0), axis=1)


def finish_kernel(arrived, out):
    slots = out.shape[1]
    places = arrived.shape[0] * GROUP // ROWS
    shape = (arrived.shape[0], GROUP, GROUP * CELLS)
    keep = iota(shape, 2) // CELLS == iota(shape, 1)
    rows = jnp.where(keep, arrived[...][:, None, :], 0.0).reshape(places * ROWS, GROUP * CELLS)
    shape = (GROUP * CELLS, slots)
    spread = (cell_of(iota(shape, 1)) == iota(shape, 0) % CELLS).astype(jnp.float32)
    wide = exact_dot(rows, spread).reshape(places, ROWS, slots)
    u, v, to = (iota(wide.shape, axis) for axis in range(3))
    target = v % COUNT
    core = (u ^ jnp.where((target == 1) | (target == 3), 1, 0)) & 1
    low = (u ^ jnp.where((target == 2) | (target == 3), 8, 0)) & 8
    across = (u + jnp.where(target == 4, 2, 0)) & 6
    here = (core + low + across == place_of(to)) | (v >= 2 * COUNT)
    result = jnp.sum(jnp.where(here, wide, 0.0), axis=0)
    alive = result[0:1] > NEVER - 1.0
    best = jnp.max(result[0:COUNT], axis=0, keepdims=True)
    nearest = jnp.where(alive, best, 0.0)
    cosine = jnp.sum(result[COUNT : 2 * COUNT], axis=0, keepdims=True) * lax.rsqrt(
        result[2 * COUNT : 2 * COUNT + 1] + EPSILON
    )
    distance = jnp.where(alive, 1.0 - cosine, 0.0)
    out[...] = jnp.concatenate([nearest, distance])


def on_chip(kernel, out_shape, flops, *operands):
    vmem = pl.BlockSpec(memory_space=pltpu.VMEM)
    single = isinstance(out_shape, jax.ShapeDtypeStruct)
    return pl.pallas_call(
        kernel,
        out_shape=out_shape,
        in_specs=[vmem] * len(operands),
        out_specs=vmem if single else [vmem] * len(out_shape),
        compiler_params=pltpu.CompilerParams(vmem_limit_bytes=16 * 2**20),
        cost_estimate=pl.CostEstimate(
            flops=flops, bytes_accessed=sum(x.size * 2 for x in operands), transcendentals=0
        ),
    )(*operands)


def local(embeddings, assignment):
    home = ("yl", "x", "core")
    far_y = lax.axis_size("yh")
    n = lax.axis_size("z")
    places = len(PLACES)
    owners = far_y * places
    width = embeddings.shape[1]
    per_owner = 2 * embeddings.shape[0] // owners
    slots = owners * per_owner
    rows = embeddings.shape[0]
    send = on_chip(
        send_kernel,
        jax.ShapeDtypeStruct((slots, width), jnp.bfloat16),
        2 * slots * rows * width,
        embeddings,
        assignment.reshape(1, rows),
    )
    own = lax.all_to_all(
        send.reshape(owners, per_owner, width),
        ("yh", "z"),
        split_axis=0,
        concat_axis=0,
        tiled=True,
    ).reshape(slots, width)
    tile = 2 * slots * slots * width
    x1 = from_place(own, X1)
    y = from_place(own, Y)
    x2 = from_place(x1, X1)
    stats = jax.ShapeDtypeStruct((8, slots), jnp.float32)
    near = on_chip(near_kernel, stats, 6 * tile, own, y, x1)
    first, later, near = lax.optimization_barrier((own, y, near))
    c = from_place(first, C)
    yc = from_place(later, C)
    seen = on_chip(far_kernel, stats, 2 * tile, near, own, y, x2)
    message = on_chip(
        last_kernel,
        jax.ShapeDtypeStruct((n * ROWS // GROUP, GROUP * CELLS), jnp.float32),
        8 * tile,
        seen,
        own,
        y,
        c,
        yc,
        x1,
        x2,
    )
    message = message.reshape(n, ROWS // GROUP, GROUP * CELLS)
    message = lax.all_to_all(message, home, split_axis=0, concat_axis=0, tiled=True)
    found = on_chip(
        finish_kernel,
        jax.ShapeDtypeStruct((2, slots), jnp.float32),
        0,
        message.reshape(places * ROWS // GROUP, GROUP * CELLS),
    )
    pairs = [(u * n + z, z * n + u) for u in range(places) for z in range(n)]
    found = lax.ppermute(found, home + ("z",), pairs)
    return found[0].reshape(1, 1, slots), found[1].reshape(1, 1, slots)


def solution(mesh):
    names = ("yh", "yl", "x", "core", "z")
    n = mesh.shape["split"]
    parts = Mesh(mesh.devices.reshape(-1, *HOME, n), names)
    in_specs = (P(names, None), P(names))
    out_specs = (P(names[:4], "z", None), P(names[:4], "z", None))
    return jax.shard_map(local, mesh=parts, in_specs=in_specs, out_specs=out_specs, check_vma=False)
```

```python
import itertools

import jax
import jax.numpy as jnp
from jax import lax
from jax.experimental import pallas as pl
from jax.experimental.pallas import tpu as pltpu
from jax.sharding import Mesh
from jax.sharding import PartitionSpec as P

EPSILON = 1e-06
NEVER = -2.0
DEAD_MARK = 2.0


DEAD_BEST = -8.0
ROWS = 16
HOME = (2, 4, 2)
OWN, C, Y, YC = (0, 0, 0), (0, 0, 1), (1, 0, 0), (1, 0, 1)
X1, X2 = (0, 1, 0), (0, 2, 0)
TARGETS = (OWN, C, Y, YC, X1)
COUNT = len(TARGETS)


def plus(a, b):
    return tuple((x + y) % d for x, y, d in zip(a, b, HOME))


def number(place):
    return (place[0] * HOME[1] + place[1]) * HOME[2] + place[2]


PLACES = list(itertools.product(*[range(d) for d in HOME]))


def from_place(value, d):
    pairs = [(number(plus(u, d)), number(u)) for u in PLACES]
    return lax.ppermute(value, ("yl", "x", "core"), pairs)


def dots(a, b):
    return lax.dot_general(a, b, (((1,), (1,)), ((), ())), preferred_element_type=jnp.float32)


def best_and_sum(far, rows, diagonal=False):
    alive = far[:, 0:1].astype(jnp.float32) < 1.5
    scores = dots(far, rows)
    total = jnp.sum(jnp.where(alive, scores, 0.0), axis=0, keepdims=True)
    if diagonal:
        same = lax.broadcasted_iota(jnp.int32, scores.shape, 0) == lax.broadcasted_iota(
            jnp.int32, scores.shape, 1
        )
        scores = jnp.where(same, NEVER, scores)
    return jnp.max(jnp.where(alive, scores, NEVER), axis=0, keepdims=True), total


def send_kernel(embeddings, assignment, out):
    values = embeddings[...].astype(jnp.float32)
    scale = lax.rsqrt(jnp.sum(values * values, axis=1, keepdims=True) + EPSILON)
    normed = (values * scale).astype(jnp.bfloat16)
    rows, slots = values.shape[0], out.shape[0]
    cluster = assignment[...]
    along = jnp.broadcast_to(cluster.astype(jnp.float32), (rows, rows))
    earlier = iota((rows, rows), 0) < iota((rows, rows), 1)
    rank = jnp.sum(jnp.where((along == along.T) & earlier, 1.0, 0.0), axis=0, keepdims=True)
    slot = (cluster % 16 * 4 + cluster // 16) * (slots // 64) + rank.astype(jnp.int32)
    table = (slot == iota((slots, rows), 0)).astype(jnp.float32)
    placed = jnp.dot(table.astype(jnp.bfloat16), normed, preferred_element_type=jnp.float32)
    empty = jnp.sum(table, axis=1, keepdims=True) < 0.5
    mark = empty & (iota(placed.shape, 1) == 0)
    out[...] = jnp.where(mark, DEAD_MARK, placed).astype(jnp.bfloat16)


def merge(old, new):
    return (jnp.maximum(old[0], new[0]), old[1] + new[1])


def near_kernel(own, c, y, x1, out):
    a, b, d, e = own[...], c[...], y[...], x1[...]
    stats = [
        merge(merge(best_and_sum(a, a, True), best_and_sum(b, a)), merge(best_and_sum(d, a), best_and_sum(e, a))),
        best_and_sum(e, b),
        best_and_sum(e, d),
        merge(merge(best_and_sum(a, e), best_and_sum(b, e)), best_and_sum(d, e)),
    ]
    out[...] = jnp.concatenate([b for b, _ in stats] + [t for _, t in stats])


def far_kernel(near, own, c, y, x2, out):
    far = x2[...]
    late = [best_and_sum(far, x[...]) for x in (own, c, y)]
    best = jnp.maximum(near[0:3, :], jnp.concatenate([b for b, _ in late]))
    total = near[4:7, :] + jnp.concatenate([t for _, t in late])
    out[...] = jnp.concatenate([best, near[3:4, :], total, near[7:8, :]])


def iota(shape, axis):
    return lax.broadcasted_iota(jnp.int32, shape, axis)


def exact_dot(a, b):
    return lax.dot_general(
        a,
        b,
        (((1,), (0,)), ((), ())),
        precision=lax.Precision.HIGHEST,
        preferred_element_type=jnp.float32,
    )


GROUP = 8
CELLS = 16


def owner_cell(slot):
    return slot // 64 * 4 + slot % 4


def owner_place(slot):
    return slot // 4 % 16


def last_kernel(seen, own, c, y, yc, x1, x2, out):
    held = [own[...], c[...], y[...], yc[...], x1[...]]
    far = x2[...]
    stats = [
        merge(best_and_sum(held[3], held[0]), (seen[0:1, :], seen[4:5, :])),
        (seen[1:2, :], seen[5:6, :]),
        (seen[2:3, :], seen[6:7, :]),
        merge(best_and_sum(held[4], held[3]), best_and_sum(far, held[3])),
        merge(best_and_sum(held[3], held[4]), (seen[3:4, :], seen[7:8, :])),
    ]
    best = jnp.concatenate([b for b, _ in stats])
    total = jnp.concatenate([t for _, t in stats])
    slots = best.shape[1]
    first = (iota((8, own.shape[1]), 1) == 0).astype(jnp.bfloat16)
    alive = jnp.concatenate([dots(first, x)[0:1] for x in held]) < 1.5
    square = jnp.sum(jnp.where(alive, total, 0.0))
    best = jnp.concatenate([jnp.where(alive[0:1], best[0:1], DEAD_BEST), best[1:]], axis=0)
    values = jnp.concatenate(
        [best, total, jnp.full((ROWS - 2 * COUNT, slots), square, jnp.float32)], axis=0
    )
    n = out.shape[0] * GROUP // ROWS
    shape = (n, ROWS, slots)
    chosen = jnp.where(iota(shape, 2) // CELLS == iota(shape, 0), values[None], 0.0)
    shape = (slots, GROUP * CELLS)
    spread = (iota(shape, 0) % CELLS == iota(shape, 1) % CELLS).astype(jnp.float32)
    wide = exact_dot(chosen.reshape(n * ROWS, slots), spread).reshape(-1, GROUP, GROUP * CELLS)
    keep = iota(wide.shape, 2) // CELLS == iota(wide.shape, 1)
    out[...] = jnp.sum(jnp.where(keep, wide, 0.0), axis=1)


def finish_kernel(arrived, out):
    slots = out.shape[1]
    places = arrived.shape[0] * GROUP // ROWS
    shape = (arrived.shape[0], GROUP, GROUP * CELLS)
    keep = iota(shape, 2) // CELLS == iota(shape, 1)
    rows = jnp.where(keep, arrived[...][:, None, :], 0.0).reshape(places * ROWS, GROUP * CELLS)
    shape = (GROUP * CELLS, slots)
    spread = (owner_cell(iota(shape, 1)) == iota(shape, 0) % CELLS).astype(jnp.float32)
    wide = exact_dot(rows, spread).reshape(places, ROWS, slots)
    u, v, to = (iota(wide.shape, axis) for axis in range(3))
    target = v % COUNT
    core = (u ^ jnp.where((target == 1) | (target == 3), 1, 0)) & 1
    low = (u ^ jnp.where((target == 2) | (target == 3), 8, 0)) & 8
    across = (u + jnp.where(target == 4, 2, 0)) & 6
    here = (core + low + across == owner_place(to)) | (v >= 2 * COUNT)
    result = jnp.sum(jnp.where(here, wide, 0.0), axis=0)
    alive = result[0:1] > NEVER - 1.0
    best = jnp.max(result[0:COUNT], axis=0, keepdims=True)
    nearest = jnp.where(alive, best, 0.0)
    cosine = jnp.sum(result[COUNT : 2 * COUNT], axis=0, keepdims=True) * lax.rsqrt(
        result[2 * COUNT : 2 * COUNT + 1] + EPSILON
    )
    distance = jnp.where(alive, 1.0 - cosine, 0.0)
    out[...] = jnp.concatenate([nearest, distance])


def on_chip(kernel, out_shape, flops, *operands):
    vmem = pl.BlockSpec(memory_space=pltpu.VMEM)
    single = isinstance(out_shape, jax.ShapeDtypeStruct)
    return pl.pallas_call(
        kernel,
        out_shape=out_shape,
        in_specs=[vmem] * len(operands),
        out_specs=vmem if single else [vmem] * len(out_shape),
        compiler_params=pltpu.CompilerParams(vmem_limit_bytes=16 * 2**20),
        cost_estimate=pl.CostEstimate(
            flops=flops, bytes_accessed=sum(x.size * 2 for x in operands), transcendentals=0
        ),
    )(*operands)


def local(embeddings, assignment):
    home = ("yl", "x", "core")
    far_y = lax.axis_size("yh")
    n = lax.axis_size("z")
    places = len(PLACES)
    owners = far_y * places
    width = embeddings.shape[1]
    per_owner = 2 * embeddings.shape[0] // owners
    slots = owners * per_owner
    rows = embeddings.shape[0]
    send = on_chip(
        send_kernel,
        jax.ShapeDtypeStruct((slots, width), jnp.bfloat16),
        2 * slots * rows * width,
        embeddings,
        assignment.reshape(1, rows),
    )
    own = lax.all_to_all(
        send.reshape(owners, per_owner, width),
        ("z", "yh"),
        split_axis=0,
        concat_axis=0,
        tiled=True,
    ).reshape(slots, width)
    tile = 2 * slots * slots * width
    x1 = from_place(own, X1)
    y = from_place(own, Y)
    x2 = from_place(x1, X1)
    stats = jax.ShapeDtypeStruct((8, slots), jnp.float32)
    c = from_place(own, C)
    near = on_chip(near_kernel, stats, 9 * tile, own, c, y, x1)
    later, near = lax.optimization_barrier((y, near))
    yc = from_place(later, C)
    seen = on_chip(far_kernel, stats, 3 * tile, near, own, c, y, x2)
    message = on_chip(
        last_kernel,
        jax.ShapeDtypeStruct((n * ROWS // GROUP, GROUP * CELLS), jnp.float32),
        4 * tile,
        seen,
        own,
        c,
        y,
        yc,
        x1,
        x2,
    )
    message = message.reshape(n, ROWS // GROUP, GROUP * CELLS)
    message = lax.all_to_all(message, home, split_axis=0, concat_axis=0, tiled=True)
    found = on_chip(
        finish_kernel,
        jax.ShapeDtypeStruct((2, slots), jnp.float32),
        0,
        message.reshape(places * ROWS // GROUP, GROUP * CELLS),
    )
    pairs = [(u * n + z, z * n + u) for u in range(places) for z in range(n)]
    found = lax.ppermute(found, home + ("z",), pairs)
    return found[0].reshape(1, 1, slots), found[1].reshape(1, 1, slots)


def solution(mesh):
    names = ("yh", "yl", "x", "core", "z")
    n = mesh.shape["split"]
    parts = Mesh(mesh.devices.reshape(-1, *HOME, n), names)
    in_specs = (P(names, None), P(names))
    out_specs = (P(names[:4], "z", None), P(names[:4], "z", None))
    return jax.shard_map(local, mesh=parts, in_specs=in_specs, out_specs=out_specs, check_vma=False)
```

```python
import itertools

import jax
import jax.numpy as jnp
from jax import lax
from jax.experimental import pallas as pl
from jax.experimental.pallas import tpu as pltpu
from jax.sharding import Mesh
from jax.sharding import PartitionSpec as P

EPSILON = 1e-06
NEVER = -2.0
DEAD_MARK = 2.0


DEAD_BEST = -8.0
ROWS = 16
HOME = (2, 4, 2)
OWN, C, Y, YC = (0, 0, 0), (0, 0, 1), (1, 0, 0), (1, 0, 1)
X1, X2 = (0, 1, 0), (0, 2, 0)
TARGETS = (OWN, C, Y, YC, X1)
COUNT = len(TARGETS)


def plus(a, b):
    return tuple((x + y) % d for x, y, d in zip(a, b, HOME))


def number(place):
    return (place[0] * HOME[1] + place[1]) * HOME[2] + place[2]


PLACES = list(itertools.product(*[range(d) for d in HOME]))


def steps_to(place):
    return place[0] + min(place[1], HOME[1] - place[1])


N = 16
OFFSETS = dict(
    zip(
        sorted(PLACES, key=lambda d: (steps_to(d), d)),
        sorted(range(N), key=lambda o: (-min(o, N - o), o)),
    )
)


def from_place(value, d):
    pairs = [(number(plus(u, d)), number(u)) for u in PLACES]
    return lax.ppermute(value, ("yl", "x", "core"), pairs)


def dots(a, b):
    return lax.dot_general(a, b, (((1,), (1,)), ((), ())), preferred_element_type=jnp.float32)


def best_and_sum(far, rows, diagonal=False):
    alive = far[:, 0:1].astype(jnp.float32) < 1.5
    scores = dots(far, rows)
    total = jnp.sum(jnp.where(alive, scores, 0.0), axis=0, keepdims=True)
    if diagonal:
        same = lax.broadcasted_iota(jnp.int32, scores.shape, 0) == lax.broadcasted_iota(
            jnp.int32, scores.shape, 1
        )
        scores = jnp.where(same, NEVER, scores)
    return jnp.max(jnp.where(alive, scores, NEVER), axis=0, keepdims=True), total


def send_kernel(embeddings, assignment, out):
    values = embeddings[...].astype(jnp.float32)
    scale = lax.rsqrt(jnp.sum(values * values, axis=1, keepdims=True) + EPSILON)
    normed = (values * scale).astype(jnp.bfloat16)
    rows, slots = values.shape[0], out.shape[0]
    along = jnp.broadcast_to(assignment[...].astype(jnp.float32), (rows, rows))
    earlier = iota((rows, rows), 0) < iota((rows, rows), 1)
    rank = jnp.sum(jnp.where((along == along.T) & earlier, 1.0, 0.0), axis=0, keepdims=True)
    slot = along[0:1] * (slots // 64) + rank
    table = (slot == iota((slots, rows), 0).astype(jnp.float32)).astype(jnp.float32)
    placed = jnp.dot(table.astype(jnp.bfloat16), normed, preferred_element_type=jnp.float32)
    empty = jnp.sum(table, axis=1, keepdims=True) < 0.5
    mark = empty & (iota(placed.shape, 1) == 0)
    out[...] = jnp.where(mark, DEAD_MARK, placed).astype(jnp.bfloat16)


def merge(old, new):
    return (jnp.maximum(old[0], new[0]), old[1] + new[1])


def near_kernel(own, y, x1, out):
    a, b, d = own[...], y[...], x1[...]
    stats = [
        merge(merge(best_and_sum(a, a, True), best_and_sum(b, a)), best_and_sum(d, a)),
        best_and_sum(d, b),
        merge(best_and_sum(a, d), best_and_sum(b, d)),
    ]
    out[...] = jnp.concatenate([b for b, _ in stats] + [t for _, t in stats] + [stats[0][0]] * 2)


def far_kernel(near, own, y, x2, out):
    far = x2[...]
    a, b = best_and_sum(far, own[...]), best_and_sum(far, y[...])
    best = jnp.maximum(near[0:2, :], jnp.concatenate([a[0], b[0]]))
    total = near[3:5, :] + jnp.concatenate([a[1], b[1]])
    out[...] = jnp.concatenate([best, near[2:3, :], total, near[5:8, :]])


def iota(shape, axis):
    return lax.broadcasted_iota(jnp.int32, shape, axis)


def exact_dot(a, b):
    return lax.dot_general(
        a,
        b,
        (((1,), (0,)), ((), ())),
        precision=lax.Precision.HIGHEST,
        preferred_element_type=jnp.float32,
    )


GROUP = 8
CELLS = 16


def cell_of(slot):
    return slot // 64 * 4 + slot % 4


def place_of(slot):
    return slot // 4 % 16


def member_for(plane, z):
    offset = (plane - z) % N
    d = sum(jnp.where(offset == o, number(d), 0) for d, o in OFFSETS.items())
    low, across, core = d // 8, d // 2 % 4, d % 2
    return (z // 8 ^ low) * 8 + (z // 2 + across) % 4 * 2 + (z ^ core) % 2


def last_kernel(z, seen, own, y, c, yc, x1, x2, out):
    held = [own[...], c[...], y[...], yc[...], x1[...]]
    far = x2[...]
    stats = [
        merge(best_and_sum(held[1], held[0]), best_and_sum(held[3], held[0])),
        merge(best_and_sum(held[4], held[1]), best_and_sum(far, held[1])),
        (seen[1:2, :], seen[4:5, :]),
        merge(best_and_sum(held[4], held[3]), best_and_sum(far, held[3])),
        merge(best_and_sum(held[1], held[4]), best_and_sum(held[3], held[4])),
    ]
    stats[0] = merge(stats[0], (seen[0:1, :], seen[3:4, :]))
    stats[4] = merge(stats[4], (seen[2:3, :], seen[5:6, :]))
    best = jnp.concatenate([b for b, _ in stats])
    total = jnp.concatenate([t for _, t in stats])
    slots = best.shape[1]
    first = (iota((8, own.shape[1]), 1) == 0).astype(jnp.bfloat16)
    alive = jnp.concatenate([dots(first, x)[0:1] for x in held]) < 1.5
    square = jnp.sum(jnp.where(alive, total, 0.0))
    best = jnp.concatenate([jnp.where(alive[0:1], best[0:1], DEAD_BEST), best[1:]], axis=0)
    values = jnp.concatenate(
        [best, total, jnp.full((ROWS - 2 * COUNT, slots), square, jnp.float32)], axis=0
    )
    n = out.shape[0] * GROUP // ROWS
    shape = (n, ROWS, slots)
    member = member_for(place_of(iota((1, slots), 1)), z[0])
    chosen = jnp.where(member[None] == iota(shape, 0), values[None], 0.0)
    shape = (slots, GROUP * CELLS)
    spread = (cell_of(iota(shape, 0)) == iota(shape, 1) % CELLS).astype(jnp.float32)
    wide = exact_dot(chosen.reshape(n * ROWS, slots), spread).reshape(-1, GROUP, GROUP * CELLS)
    keep = iota(wide.shape, 2) // CELLS == iota(wide.shape, 1)
    out[...] = jnp.sum(jnp.where(keep, wide, 0.0), axis=1)


def finish_kernel(arrived, out):
    slots = out.shape[1]
    places = arrived.shape[0] * GROUP // ROWS
    shape = (arrived.shape[0], GROUP, GROUP * CELLS)
    keep = iota(shape, 2) // CELLS == iota(shape, 1)
    rows = jnp.where(keep, arrived[...][:, None, :], 0.0).reshape(places * ROWS, GROUP * CELLS)
    shape = (GROUP * CELLS, slots)
    spread = (cell_of(iota(shape, 1)) == iota(shape, 0) % CELLS).astype(jnp.float32)
    wide = exact_dot(rows, spread).reshape(places, ROWS, slots)
    u, v, to = (iota(wide.shape, axis) for axis in range(3))
    target = v % COUNT
    core = (u ^ jnp.where((target == 1) | (target == 3), 1, 0)) & 1
    low = (u ^ jnp.where((target == 2) | (target == 3), 8, 0)) & 8
    across = (u + jnp.where(target == 4, 2, 0)) & 6
    here = (core + low + across == place_of(to)) | (v >= 2 * COUNT)
    result = jnp.sum(jnp.where(here, wide, 0.0), axis=0)
    alive = result[0:1] > NEVER - 1.0
    best = jnp.max(result[0:COUNT], axis=0, keepdims=True)
    nearest = jnp.where(alive, best, 0.0)
    cosine = jnp.sum(result[COUNT : 2 * COUNT], axis=0, keepdims=True) * lax.rsqrt(
        result[2 * COUNT : 2 * COUNT + 1] + EPSILON
    )
    distance = jnp.where(alive, 1.0 - cosine, 0.0)
    out[...] = jnp.concatenate([nearest, distance])


def on_chip(kernel, out_shape, flops, *operands):
    vmem = pl.BlockSpec(memory_space=pltpu.VMEM)
    smem = pl.BlockSpec(memory_space=pltpu.SMEM)
    return pl.pallas_call(
        kernel,
        out_shape=out_shape,
        in_specs=[smem if x.size == 1 else vmem for x in operands],
        out_specs=vmem,
        compiler_params=pltpu.CompilerParams(vmem_limit_bytes=16 * 2**20),
        cost_estimate=pl.CostEstimate(
            flops=flops, bytes_accessed=sum(x.size * 2 for x in operands), transcendentals=0
        ),
    )(*operands)


def local(embeddings, assignment):
    home = ("yl", "x", "core")
    far_y = lax.axis_size("yh")
    n = lax.axis_size("z")
    places = len(PLACES)
    owners = far_y * places
    width = embeddings.shape[1]
    per_owner = 2 * embeddings.shape[0] // owners
    slots = owners * per_owner
    rows = embeddings.shape[0]
    send = on_chip(
        send_kernel,
        jax.ShapeDtypeStruct((slots, width), jnp.bfloat16),
        2 * slots * rows * width,
        embeddings,
        assignment.reshape(1, rows),
    )
    own = lax.all_to_all(
        send.reshape(owners, per_owner, width),
        ("yh", "z"),
        split_axis=0,
        concat_axis=0,
        tiled=True,
    ).reshape(slots, width)
    tile = 2 * slots * slots * width
    x1 = from_place(own, X1)
    y = from_place(own, Y)
    x2 = from_place(x1, X1)
    stats = jax.ShapeDtypeStruct((8, slots), jnp.float32)
    near = on_chip(near_kernel, stats, 6 * tile, own, y, x1)
    first, later, near = lax.optimization_barrier((own, y, near))
    c = from_place(first, C)
    yc = from_place(later, C)
    seen = on_chip(far_kernel, stats, 2 * tile, near, own, y, x2)
    message = on_chip(
        last_kernel,
        jax.ShapeDtypeStruct((n * ROWS // GROUP, GROUP * CELLS), jnp.float32),
        8 * tile,
        lax.axis_index("z").astype(jnp.int32).reshape(1),
        seen,
        own,
        y,
        c,
        yc,
        x1,
        x2,
    )
    message = message.reshape(n, ROWS // GROUP, GROUP * CELLS)
    message = lax.all_to_all(message, home, split_axis=0, concat_axis=0, tiled=True)
    found = on_chip(
        finish_kernel,
        jax.ShapeDtypeStruct((2, slots), jnp.float32),
        0,
        message.reshape(places * ROWS // GROUP, GROUP * CELLS),
    )
    pairs = []
    for z in range(n):
        for d, offset in OFFSETS.items():
            pairs.append((number(plus(PLACES[z], d)) * n + z, z * n + (z + offset) % n))
    found = lax.ppermute(found, home + ("z",), pairs)
    return found[0].reshape(1, 1, slots), found[1].reshape(1, 1, slots)


def solution(mesh):
    names = ("yh", "yl", "x", "core", "z")
    n = mesh.shape["split"]
    parts = Mesh(mesh.devices.reshape(-1, *HOME, n), names)
    in_specs = (P(names, None), P(names))
    out_specs = (P(names[:4], "z", None), P(names[:4], "z", None))
    return jax.shard_map(local, mesh=parts, in_specs=in_specs, out_specs=out_specs, check_vma=False)
```

```python
import itertools

import jax
import jax.numpy as jnp
from jax import lax
from jax.experimental import pallas as pl
from jax.experimental.pallas import tpu as pltpu
from jax.sharding import Mesh
from jax.sharding import PartitionSpec as P

EPSILON = 1e-06
NEVER = -2.0
DEAD_MARK = 2.0


DEAD_BEST = -8.0
ROWS = 16
HOME = (2, 4, 2)
OWN, C, Y, YC = (0, 0, 0), (0, 0, 1), (1, 0, 0), (1, 0, 1)
X1, X2 = (0, 1, 0), (0, 2, 0)
TARGETS = (OWN, C, Y, YC, X1)
COUNT = len(TARGETS)


def plus(a, b):
    return tuple((x + y) % d for x, y, d in zip(a, b, HOME))


def number(place):
    return (place[1] * HOME[0] + place[0]) * HOME[2] + place[2]


PLACES = list(itertools.product(*[range(d) for d in HOME]))


def from_place(value, d):
    pairs = [(number(plus(u, d)), number(u)) for u in PLACES]
    return lax.ppermute(value, ("yl", "xl", "core"), pairs)


def dots(a, b):
    return lax.dot_general(a, b, (((1,), (1,)), ((), ())), preferred_element_type=jnp.float32)


def best_and_sum(far, rows, diagonal=False):
    alive = far[:, 0:1].astype(jnp.float32) < 1.5
    scores = dots(far, rows)
    total = jnp.sum(jnp.where(alive, scores, 0.0), axis=0, keepdims=True)
    if diagonal:
        same = lax.broadcasted_iota(jnp.int32, scores.shape, 0) == lax.broadcasted_iota(
            jnp.int32, scores.shape, 1
        )
        scores = jnp.where(same, NEVER, scores)
    return jnp.max(jnp.where(alive, scores, NEVER), axis=0, keepdims=True), total


def send_kernel(embeddings, assignment, out):
    values = embeddings[...].astype(jnp.float32)
    scale = lax.rsqrt(jnp.sum(values * values, axis=1, keepdims=True) + EPSILON)
    normed = (values * scale).astype(jnp.bfloat16)
    rows, slots = values.shape[0], out.shape[0]
    along = jnp.broadcast_to(assignment[...].astype(jnp.float32), (rows, rows))
    earlier = iota((rows, rows), 0) < iota((rows, rows), 1)
    rank = jnp.sum(jnp.where((along == along.T) & earlier, 1.0, 0.0), axis=0, keepdims=True)
    k = assignment[...]
    low = (k // 8 % 4 * 2 + k // 2 % 2) * 2 + k % 2
    home = (k // 32 * 2 + k // 4 % 2) * 16 + low
    slot = home.astype(jnp.float32) * (slots // 64) + rank
    table = (slot == iota((slots, rows), 0).astype(jnp.float32)).astype(jnp.float32)
    placed = jnp.dot(table.astype(jnp.bfloat16), normed, preferred_element_type=jnp.float32)
    empty = jnp.sum(table, axis=1, keepdims=True) < 0.5
    mark = empty & (iota(placed.shape, 1) == 0)
    out[...] = jnp.where(mark, DEAD_MARK, placed).astype(jnp.bfloat16)


def merge(old, new):
    return (jnp.maximum(old[0], new[0]), old[1] + new[1])


def near_kernel(own, y, x1, out):
    a, b, d = own[...], y[...], x1[...]
    stats = [
        merge(merge(best_and_sum(a, a, True), best_and_sum(b, a)), best_and_sum(d, a)),
        best_and_sum(d, b),
        merge(best_and_sum(a, d), best_and_sum(b, d)),
    ]
    out[...] = jnp.concatenate([b for b, _ in stats] + [t for _, t in stats] + [stats[0][0]] * 2)


def far_kernel(near, own, y, x2, out):
    far = x2[...]
    a, b = best_and_sum(far, own[...]), best_and_sum(far, y[...])
    best = jnp.maximum(near[0:2, :], jnp.concatenate([a[0], b[0]]))
    total = near[3:5, :] + jnp.concatenate([a[1], b[1]])
    out[...] = jnp.concatenate([best, near[2:3, :], total, near[5:8, :]])


def iota(shape, axis):
    return lax.broadcasted_iota(jnp.int32, shape, axis)


def exact_dot(a, b):
    return lax.dot_general(
        a,
        b,
        (((1,), (0,)), ((), ())),
        precision=lax.Precision.HIGHEST,
        preferred_element_type=jnp.float32,
    )


GROUP = 8
CELLS = 16


def cell_of(slot):
    return slot // 64 * 4 + slot % 4


def place_of(slot):
    return slot // 4 % 16


def owner_cell(slot):
    return (slot // 128 * 2 + slot // 16 % 2) * 4 + slot % 4


def owner_place(slot):
    return (slot // 32 % 4 * 2 + slot // 8 % 2) * 2 + slot // 4 % 2


def last_kernel(seen, own, y, c, yc, x1, x2, out):
    held = [own[...], c[...], y[...], yc[...], x1[...]]
    far = x2[...]
    stats = [
        merge(best_and_sum(held[1], held[0]), best_and_sum(held[3], held[0])),
        merge(best_and_sum(held[4], held[1]), best_and_sum(far, held[1])),
        (seen[1:2, :], seen[4:5, :]),
        merge(best_and_sum(held[4], held[3]), best_and_sum(far, held[3])),
        merge(best_and_sum(held[1], held[4]), best_and_sum(held[3], held[4])),
    ]
    stats[0] = merge(stats[0], (seen[0:1, :], seen[3:4, :]))
    stats[4] = merge(stats[4], (seen[2:3, :], seen[5:6, :]))
    best = jnp.concatenate([b for b, _ in stats])
    total = jnp.concatenate([t for _, t in stats])
    slots = best.shape[1]
    first = (iota((8, own.shape[1]), 1) == 0).astype(jnp.bfloat16)
    alive = jnp.concatenate([dots(first, x)[0:1] for x in held]) < 1.5
    square = jnp.sum(jnp.where(alive, total, 0.0))
    best = jnp.concatenate([jnp.where(alive[0:1], best[0:1], DEAD_BEST), best[1:]], axis=0)
    values = jnp.concatenate(
        [best, total, jnp.full((ROWS - 2 * COUNT, slots), square, jnp.float32)], axis=0
    )
    n = out.shape[0] * GROUP // ROWS
    shape = (n, ROWS, slots)
    chosen = jnp.where(place_of(iota(shape, 2)) == iota(shape, 0), values[None], 0.0)
    shape = (slots, GROUP * CELLS)
    spread = (cell_of(iota(shape, 0)) == iota(shape, 1) % CELLS).astype(jnp.float32)
    wide = exact_dot(chosen.reshape(n * ROWS, slots), spread).reshape(-1, GROUP, GROUP * CELLS)
    keep = iota(wide.shape, 2) // CELLS == iota(wide.shape, 1)
    out[...] = jnp.sum(jnp.where(keep, wide, 0.0), axis=1)


def finish_kernel(arrived, out):
    slots = out.shape[1]
    places = arrived.shape[0] * GROUP // ROWS
    shape = (arrived.shape[0], GROUP, GROUP * CELLS)
    keep = iota(shape, 2) // CELLS == iota(shape, 1)
    rows = jnp.where(keep, arrived[...][:, None, :], 0.0).reshape(places * ROWS, GROUP * CELLS)
    shape = (GROUP * CELLS, slots)
    spread = (owner_cell(iota(shape, 1)) == iota(shape, 0) % CELLS).astype(jnp.float32)
    wide = exact_dot(rows, spread).reshape(places, ROWS, slots)
    u, v, to = (iota(wide.shape, axis) for axis in range(3))
    target = v % COUNT
    core = (u ^ jnp.where((target == 1) | (target == 3), 1, 0)) & 1
    low = (u ^ jnp.where((target == 2) | (target == 3), 2, 0)) & 2
    across = (u + jnp.where(target == 4, 4, 0)) & 12
    here = (core + low + across == owner_place(to)) | (v >= 2 * COUNT)
    result = jnp.sum(jnp.where(here, wide, 0.0), axis=0)
    alive = result[0:1] > NEVER - 1.0
    best = jnp.max(result[0:COUNT], axis=0, keepdims=True)
    nearest = jnp.where(alive, best, 0.0)
    cosine = jnp.sum(result[COUNT : 2 * COUNT], axis=0, keepdims=True) * lax.rsqrt(
        result[2 * COUNT : 2 * COUNT + 1] + EPSILON
    )
    distance = jnp.where(alive, 1.0 - cosine, 0.0)
    out[...] = jnp.concatenate([nearest, distance])


def on_chip(kernel, out_shape, flops, *operands):
    vmem = pl.BlockSpec(memory_space=pltpu.VMEM)
    single = isinstance(out_shape, jax.ShapeDtypeStruct)
    return pl.pallas_call(
        kernel,
        out_shape=out_shape,
        in_specs=[vmem] * len(operands),
        out_specs=vmem if single else [vmem] * len(out_shape),
        compiler_params=pltpu.CompilerParams(vmem_limit_bytes=16 * 2**20),
        cost_estimate=pl.CostEstimate(
            flops=flops, bytes_accessed=sum(x.size * 2 for x in operands), transcendentals=0
        ),
    )(*operands)


def local(embeddings, assignment):
    home = ("yl", "xl", "core")
    far_y = lax.axis_size("yh") * lax.axis_size("xh")
    n = lax.axis_size("z")
    places = len(PLACES)
    owners = far_y * places
    width = embeddings.shape[1]
    per_owner = 2 * embeddings.shape[0] // owners
    slots = owners * per_owner
    rows = embeddings.shape[0]
    send = on_chip(
        send_kernel,
        jax.ShapeDtypeStruct((slots, width), jnp.bfloat16),
        2 * slots * rows * width,
        embeddings,
        assignment.reshape(1, rows),
    )
    own = lax.all_to_all(
        send.reshape(owners, per_owner, width),
        ("yh", "xh", "z"),
        split_axis=0,
        concat_axis=0,
        tiled=True,
    ).reshape(slots, width)
    tile = 2 * slots * slots * width
    x1 = from_place(own, X1)
    y = from_place(own, Y)
    x2 = from_place(x1, X1)
    stats = jax.ShapeDtypeStruct((8, slots), jnp.float32)
    near = on_chip(near_kernel, stats, 6 * tile, own, y, x1)
    first, later, near = lax.optimization_barrier((own, y, near))
    c = from_place(first, C)
    yc = from_place(later, C)
    seen = on_chip(far_kernel, stats, 2 * tile, near, own, y, x2)
    message = on_chip(
        last_kernel,
        jax.ShapeDtypeStruct((n * ROWS // GROUP, GROUP * CELLS), jnp.float32),
        8 * tile,
        seen,
        own,
        y,
        c,
        yc,
        x1,
        x2,
    )
    message = message.reshape(n, ROWS // GROUP, GROUP * CELLS)
    message = lax.all_to_all(message, home, split_axis=0, concat_axis=0, tiled=True)
    found = on_chip(
        finish_kernel,
        jax.ShapeDtypeStruct((2, slots), jnp.float32),
        0,
        message.reshape(places * ROWS // GROUP, GROUP * CELLS),
    )
    pairs = [(u * n + z, z * n + u) for u in range(places) for z in range(n)]
    found = lax.ppermute(found, home + ("z",), pairs)
    return found[0].reshape(1, 1, slots), found[1].reshape(1, 1, slots)


def solution(mesh):
    names = ("yh", "yl", "xh", "xl", "core", "z")
    n = mesh.shape["split"]
    parts = Mesh(mesh.devices.reshape(-1, 4, 2, 2, 2, n), names)
    in_specs = (P(names, None), P(names))
    out_specs = (P(names[:5], "z", None), P(names[:5], "z", None))
    return jax.shard_map(local, mesh=parts, in_specs=in_specs, out_specs=out_specs, check_vma=False)
```

```python
import itertools

import jax
import jax.numpy as jnp
from jax import lax
from jax.experimental import pallas as pl
from jax.experimental.pallas import tpu as pltpu
from jax.sharding import Mesh
from jax.sharding import PartitionSpec as P

EPSILON = 1e-06
NEVER = -2.0
DEAD_MARK = 2.0


DEAD_BEST = -8.0
ROWS = 16
HOME = (2, 4, 2)
OWN, C, Y, YC = (0, 0, 0), (0, 0, 1), (1, 0, 0), (1, 0, 1)
X1, X2 = (0, 1, 0), (0, 2, 0)
TARGETS = (OWN, C, Y, YC, X1)
COUNT = len(TARGETS)


def plus(a, b):
    return tuple((x + y) % d for x, y, d in zip(a, b, HOME))


def number(place):
    return (place[0] * HOME[1] + place[1]) * HOME[2] + place[2]


PLACES = list(itertools.product(*[range(d) for d in HOME]))


def from_place(value, d):
    pairs = [(number(plus(u, d)), number(u)) for u in PLACES]
    return lax.ppermute(value, ("yl", "x", "core"), pairs)


def dots(a, b):
    return lax.dot_general(a, b, (((1,), (1,)), ((), ())), preferred_element_type=jnp.float32)


def best_and_sum(far, rows, diagonal=False):
    alive = far[:, 0:1].astype(jnp.float32) < 1.5
    scores = dots(far, rows)
    total = jnp.sum(jnp.where(alive, scores, 0.0), axis=0, keepdims=True)
    if diagonal:
        same = lax.broadcasted_iota(jnp.int32, scores.shape, 0) == lax.broadcasted_iota(
            jnp.int32, scores.shape, 1
        )
        scores = jnp.where(same, NEVER, scores)
    return jnp.max(jnp.where(alive, scores, NEVER), axis=0, keepdims=True), total


def send_kernel(embeddings, assignment, out):
    values = embeddings[...].astype(jnp.float32)
    scale = lax.rsqrt(jnp.sum(values * values, axis=1, keepdims=True) + EPSILON)
    normed = (values * scale).astype(jnp.bfloat16)
    rows, slots = values.shape[0], out.shape[0]
    along = jnp.broadcast_to(assignment[...].astype(jnp.float32), (rows, rows))
    earlier = iota((rows, rows), 0) < iota((rows, rows), 1)
    rank = jnp.sum(jnp.where((along == along.T) & earlier, 1.0, 0.0), axis=0, keepdims=True)
    slot = along[0:1] * (slots // 64) + rank
    table = (slot == iota((slots, rows), 0).astype(jnp.float32)).astype(jnp.float32)
    placed = jnp.dot(table.astype(jnp.bfloat16), normed, preferred_element_type=jnp.float32)
    empty = jnp.sum(table, axis=1, keepdims=True) < 0.5
    mark = empty & (iota(placed.shape, 1) == 0)
    out[...] = jnp.where(mark, DEAD_MARK, placed).astype(jnp.bfloat16)


def merge(old, new):
    return (jnp.maximum(old[0], new[0]), old[1] + new[1])


def near_kernel(own, y, x1, out):
    a, b, d = own[...], y[...], x1[...]
    stats = [
        merge(merge(best_and_sum(a, a, True), best_and_sum(b, a)), best_and_sum(d, a)),
        best_and_sum(d, b),
        merge(best_and_sum(a, d), best_and_sum(b, d)),
    ]
    out[...] = jnp.concatenate([b for b, _ in stats] + [t for _, t in stats] + [stats[0][0]] * 2)


def far_kernel(near, own, y, x2, out):
    far = x2[...]
    a, b = best_and_sum(far, own[...]), best_and_sum(far, y[...])
    best = jnp.maximum(near[0:2, :], jnp.concatenate([a[0], b[0]]))
    total = near[3:5, :] + jnp.concatenate([a[1], b[1]])
    out[...] = jnp.concatenate([best, near[2:3, :], total, near[5:8, :]])


def iota(shape, axis):
    return lax.broadcasted_iota(jnp.int32, shape, axis)


def exact_dot(a, b):
    return lax.dot_general(
        a,
        b,
        (((1,), (0,)), ((), ())),
        precision=lax.Precision.HIGHEST,
        preferred_element_type=jnp.float32,
    )


GROUP = 8
CELLS = 16


def cell_of(slot):
    return slot // 64 * 4 + slot % 4


def place_of(slot):
    return slot // 4 % 16


def last_kernel(seen, own, y, c, yc, x1, x2, out):
    held = [own[...], c[...], y[...], yc[...], x1[...]]
    far = x2[...]
    stats = [
        merge(best_and_sum(held[1], held[0]), best_and_sum(held[3], held[0])),
        merge(best_and_sum(held[4], held[1]), best_and_sum(far, held[1])),
        (seen[1:2, :], seen[4:5, :]),
        merge(best_and_sum(held[4], held[3]), best_and_sum(far, held[3])),
        merge(best_and_sum(held[1], held[4]), best_and_sum(held[3], held[4])),
    ]
    stats[0] = merge(stats[0], (seen[0:1, :], seen[3:4, :]))
    stats[4] = merge(stats[4], (seen[2:3, :], seen[5:6, :]))
    best = jnp.concatenate([b for b, _ in stats])
    total = jnp.concatenate([t for _, t in stats])
    slots = best.shape[1]
    first = (iota((8, own.shape[1]), 1) == 0).astype(jnp.bfloat16)
    alive = jnp.concatenate([dots(first, x)[0:1] for x in held]) < 1.5
    square = jnp.sum(jnp.where(alive, total, 0.0))
    best = jnp.concatenate([jnp.where(alive[0:1], best[0:1], DEAD_BEST), best[1:]], axis=0)
    values = jnp.concatenate(
        [best, total, jnp.full((ROWS - 2 * COUNT, slots), square, jnp.float32)], axis=0
    )
    n = out.shape[0] * GROUP // ROWS
    shape = (n, ROWS, slots)
    chosen = jnp.where(place_of(iota(shape, 2)) == iota(shape, 0), values[None], 0.0)
    shape = (slots, GROUP * CELLS)
    spread = (cell_of(iota(shape, 0)) == iota(shape, 1) % CELLS).astype(jnp.float32)
    wide = exact_dot(chosen.reshape(n * ROWS, slots), spread).reshape(-1, GROUP, GROUP * CELLS)
    keep = iota(wide.shape, 2) // CELLS == iota(wide.shape, 1)
    out[...] = jnp.sum(jnp.where(keep, wide, 0.0), axis=1)


def finish_kernel(arrived, out):
    slots = out.shape[1]
    places = arrived.shape[0] * GROUP // ROWS
    shape = (arrived.shape[0], GROUP, GROUP * CELLS)
    keep = iota(shape, 2) // CELLS == iota(shape, 1)
    rows = jnp.where(keep, arrived[...][:, None, :], 0.0).reshape(places * ROWS, GROUP * CELLS)
    shape = (GROUP * CELLS, slots)
    spread = (cell_of(iota(shape, 1)) == iota(shape, 0) % CELLS).astype(jnp.float32)
    wide = exact_dot(rows, spread).reshape(places, ROWS, slots)
    u, v, to = (iota(wide.shape, axis) for axis in range(3))
    target = v % COUNT
    core = (u ^ jnp.where((target == 1) | (target == 3), 1, 0)) & 1
    low = (u ^ jnp.where((target == 2) | (target == 3), 8, 0)) & 8
    across = (u + jnp.where(target == 4, 2, 0)) & 6
    here = (core + low + across == place_of(to)) | (v >= 2 * COUNT)
    result = jnp.sum(jnp.where(here, wide, 0.0), axis=0)
    alive = result[0:1] > NEVER - 1.0
    best = jnp.max(result[0:COUNT], axis=0, keepdims=True)
    nearest = jnp.where(alive, best, 0.0)
    square = jnp.maximum(result[2 * COUNT : 2 * COUNT + 1], 0.0)
    total = jnp.sum(result[COUNT : 2 * COUNT], axis=0, keepdims=True)
    cosine = total * lax.rsqrt(square + EPSILON)
    distance = jnp.where(alive, 1.0 - cosine, 0.0)
    out[...] = jnp.concatenate([nearest, distance])


def on_chip(kernel, out_shape, flops, *operands):
    vmem = pl.BlockSpec(memory_space=pltpu.VMEM)
    single = isinstance(out_shape, jax.ShapeDtypeStruct)
    return pl.pallas_call(
        kernel,
        out_shape=out_shape,
        in_specs=[vmem] * len(operands),
        out_specs=vmem if single else [vmem] * len(out_shape),
        compiler_params=pltpu.CompilerParams(vmem_limit_bytes=16 * 2**20),
        cost_estimate=pl.CostEstimate(
            flops=flops, bytes_accessed=sum(x.size * 2 for x in operands), transcendentals=0
        ),
    )(*operands)


def local(embeddings, assignment):
    home = ("yl", "x", "core")
    far_y = lax.axis_size("yh")
    n = lax.axis_size("z")
    places = len(PLACES)
    owners = far_y * places
    width = embeddings.shape[1]
    per_owner = 2 * embeddings.shape[0] // owners
    slots = owners * per_owner
    rows = embeddings.shape[0]
    send = on_chip(
        send_kernel,
        jax.ShapeDtypeStruct((slots, width), jnp.bfloat16),
        2 * slots * rows * width,
        embeddings,
        assignment.reshape(1, rows),
    )
    own = lax.all_to_all(
        send.reshape(owners, per_owner, width),
        ("yh", "z"),
        split_axis=0,
        concat_axis=0,
        tiled=True,
    ).reshape(slots, width)
    tile = 2 * slots * slots * width
    x1 = from_place(own, X1)
    y = from_place(own, Y)
    x2 = from_place(x1, X1)
    stats = jax.ShapeDtypeStruct((8, slots), jnp.float32)
    near = on_chip(near_kernel, stats, 6 * tile, own, y, x1)
    first, later, near = lax.optimization_barrier((own, y, near))
    c = from_place(first, C)
    yc = from_place(later, C)
    seen = on_chip(far_kernel, stats, 2 * tile, near, own, y, x2)
    message = on_chip(
        last_kernel,
        jax.ShapeDtypeStruct((n * ROWS // GROUP, GROUP * CELLS), jnp.float32),
        8 * tile,
        seen,
        own,
        y,
        c,
        yc,
        x1,
        x2,
    )
    message = message.reshape(n, ROWS // GROUP, GROUP * CELLS)
    message = lax.all_to_all(message, home, split_axis=0, concat_axis=0, tiled=True)
    found = on_chip(
        finish_kernel,
        jax.ShapeDtypeStruct((2, slots), jnp.float32),
        0,
        message.reshape(places * ROWS // GROUP, GROUP * CELLS),
    )
    pairs = [(u * n + z, z * n + u) for u in range(places) for z in range(n)]
    found = lax.ppermute(found, home + ("z",), pairs)
    return found[0].reshape(1, 1, slots), found[1].reshape(1, 1, slots)


def solution(mesh):
    names = ("yh", "yl", "x", "core", "z")
    n = mesh.shape["split"]
    parts = Mesh(mesh.devices.reshape(-1, *HOME, n), names)
    in_specs = (P(names, None), P(names))
    out_specs = (P(names[:4], "z", None), P(names[:4], "z", None))
    return jax.shard_map(local, mesh=parts, in_specs=in_specs, out_specs=out_specs, check_vma=False)
```

```python
import itertools

import jax
import jax.numpy as jnp
from jax import lax
from jax.experimental import pallas as pl
from jax.experimental.pallas import tpu as pltpu
from jax.sharding import Mesh
from jax.sharding import PartitionSpec as P

EPSILON = 1e-06
NEVER = -2.0
DEAD_MARK = 2.0


DEAD_BEST = -8.0
ROWS = 16
HOME = (2, 4, 2)
OWN, C, Y, YC = (0, 0, 0), (0, 0, 1), (1, 0, 0), (1, 0, 1)
X1, X2 = (0, 1, 0), (0, 2, 0)
TARGETS = (OWN, C, Y, YC, X1)
COUNT = len(TARGETS)


def plus(a, b):
    return tuple((x + y) % d for x, y, d in zip(a, b, HOME))


def number(place):
    return (place[0] * HOME[1] + place[1]) * HOME[2] + place[2]


PLACES = list(itertools.product(*[range(d) for d in HOME]))


def from_place(value, d):
    pairs = [(number(plus(u, d)), number(u)) for u in PLACES]
    return lax.ppermute(value, ("yl", "x", "core"), pairs)


def dots(a, b):
    return lax.dot_general(a, b, (((1,), (1,)), ((), ())), preferred_element_type=jnp.float32)


def best_and_sum(far, rows, diagonal=False):
    alive = far[:, 0:1].astype(jnp.float32) < 1.5
    scores = dots(far, rows)
    total = jnp.sum(jnp.where(alive, scores, 0.0), axis=0, keepdims=True)
    if diagonal:
        same = lax.broadcasted_iota(jnp.int32, scores.shape, 0) == lax.broadcasted_iota(
            jnp.int32, scores.shape, 1
        )
        scores = jnp.where(same, NEVER, scores)
    return jnp.max(jnp.where(alive, scores, NEVER), axis=0, keepdims=True), total


def send_kernel(embeddings, assignment, out):
    values = embeddings[...].astype(jnp.float32)
    scale = lax.rsqrt(jnp.sum(values * values, axis=1, keepdims=True) + EPSILON)
    normed = (values * scale).astype(jnp.bfloat16)
    rows, slots = values.shape[0], out.shape[0]
    along = jnp.broadcast_to(assignment[...].astype(jnp.float32), (rows, rows))
    earlier = iota((rows, rows), 0) < iota((rows, rows), 1)
    rank = jnp.sum(jnp.where((along == along.T) & earlier, 1.0, 0.0), axis=0, keepdims=True)
    slot = along[0:1] * (slots // 64) + rank
    table = (slot == iota((slots, rows), 0).astype(jnp.float32)).astype(jnp.float32)
    placed = jnp.dot(table.astype(jnp.bfloat16), normed, preferred_element_type=jnp.float32)
    empty = jnp.sum(table, axis=1, keepdims=True) < 0.5
    mark = empty & (iota(placed.shape, 1) == 0)
    out[...] = jnp.where(mark, DEAD_MARK, placed).astype(jnp.bfloat16)


def merge(old, new):
    return (jnp.maximum(old[0], new[0]), old[1] + new[1])


def near_kernel(own, y, x1, out):
    a, b, d = own[...], y[...], x1[...]
    stats = [
        merge(merge(best_and_sum(a, a, True), best_and_sum(b, a)), best_and_sum(d, a)),
        best_and_sum(d, b),
        merge(best_and_sum(a, d), best_and_sum(b, d)),
    ]
    first = (iota((8, own.shape[1]), 1) == 0).astype(jnp.bfloat16)
    marks = [dots(first, x)[0:1] for x in (a, b, d)]
    out[...] = jnp.concatenate(
        [b for b, _ in stats] + [t for _, t in stats] + marks + marks[0:1] * (ROWS - 9)
    )


def far_kernel(near, own, y, x2, out):
    far = x2[...]
    a, b = best_and_sum(far, own[...]), best_and_sum(far, y[...])
    best = jnp.maximum(near[0:2, :], jnp.concatenate([a[0], b[0]]))
    total = near[3:5, :] + jnp.concatenate([a[1], b[1]])
    out[...] = jnp.concatenate([best, near[2:3, :], total, near[5:ROWS, :]])


def iota(shape, axis):
    return lax.broadcasted_iota(jnp.int32, shape, axis)


def exact_dot(a, b):
    return lax.dot_general(
        a,
        b,
        (((1,), (0,)), ((), ())),
        precision=lax.Precision.HIGHEST,
        preferred_element_type=jnp.float32,
    )


GROUP = 8
CELLS = 16


def cell_of(slot):
    return slot // 64 * 4 + slot % 4


def place_of(slot):
    return slot // 4 % 16


def last_kernel(seen, own, y, c, yc, x1, x2, out):
    held = [own[...], c[...], y[...], yc[...], x1[...]]
    far = x2[...]
    stats = [
        merge(best_and_sum(held[1], held[0]), best_and_sum(held[3], held[0])),
        merge(best_and_sum(held[4], held[1]), best_and_sum(far, held[1])),
        (seen[1:2, :], seen[4:5, :]),
        merge(best_and_sum(held[4], held[3]), best_and_sum(far, held[3])),
        merge(best_and_sum(held[1], held[4]), best_and_sum(held[3], held[4])),
    ]
    stats[0] = merge(stats[0], (seen[0:1, :], seen[3:4, :]))
    stats[4] = merge(stats[4], (seen[2:3, :], seen[5:6, :]))
    best = jnp.concatenate([b for b, _ in stats])
    total = jnp.concatenate([t for _, t in stats])
    slots = best.shape[1]
    first = (iota((8, own.shape[1]), 1) == 0).astype(jnp.bfloat16)
    marks = [dots(first, x)[0:1] for x in (held[1], held[3])]
    alive = (
        jnp.concatenate([seen[6:7, :], marks[0], seen[7:8, :], marks[1], seen[8:9, :]]) < 1.5
    )
    square = jnp.sum(jnp.where(alive, total, 0.0))
    best = jnp.concatenate([jnp.where(alive[0:1], best[0:1], DEAD_BEST), best[1:]], axis=0)
    values = jnp.concatenate(
        [best, total, jnp.full((ROWS - 2 * COUNT, slots), square, jnp.float32)], axis=0
    )
    n = out.shape[0] * GROUP // ROWS
    shape = (n, ROWS, slots)
    chosen = jnp.where(place_of(iota(shape, 2)) == iota(shape, 0), values[None], 0.0)
    shape = (slots, GROUP * CELLS)
    spread = (cell_of(iota(shape, 0)) == iota(shape, 1) % CELLS).astype(jnp.float32)
    wide = exact_dot(chosen.reshape(n * ROWS, slots), spread).reshape(-1, GROUP, GROUP * CELLS)
    keep = iota(wide.shape, 2) // CELLS == iota(wide.shape, 1)
    out[...] = jnp.sum(jnp.where(keep, wide, 0.0), axis=1)


def finish_kernel(arrived, out):
    slots = out.shape[1]
    places = arrived.shape[0] * GROUP // ROWS
    shape = (arrived.shape[0], GROUP, GROUP * CELLS)
    keep = iota(shape, 2) // CELLS == iota(shape, 1)
    rows = jnp.where(keep, arrived[...][:, None, :], 0.0).reshape(places * ROWS, GROUP * CELLS)
    shape = (GROUP * CELLS, slots)
    spread = (cell_of(iota(shape, 1)) == iota(shape, 0) % CELLS).astype(jnp.float32)
    wide = exact_dot(rows, spread).reshape(places, ROWS, slots)
    u, v, to = (iota(wide.shape, axis) for axis in range(3))
    target = v % COUNT
    core = (u ^ jnp.where((target == 1) | (target == 3), 1, 0)) & 1
    low = (u ^ jnp.where((target == 2) | (target == 3), 8, 0)) & 8
    across = (u + jnp.where(target == 4, 2, 0)) & 6
    here = (core + low + across == place_of(to)) | (v >= 2 * COUNT)
    result = jnp.sum(jnp.where(here, wide, 0.0), axis=0)
    alive = result[0:1] > NEVER - 1.0
    best = jnp.max(result[0:COUNT], axis=0, keepdims=True)
    nearest = jnp.where(alive, best, 0.0)
    square = jnp.maximum(result[2 * COUNT : 2 * COUNT + 1], 0.0)
    total = jnp.sum(result[COUNT : 2 * COUNT], axis=0, keepdims=True)
    cosine = total * lax.rsqrt(square + EPSILON)
    distance = jnp.where(alive, 1.0 - cosine, 0.0)
    out[...] = jnp.concatenate([nearest, distance])


def on_chip(kernel, out_shape, flops, *operands):
    vmem = pl.BlockSpec(memory_space=pltpu.VMEM)
    single = isinstance(out_shape, jax.ShapeDtypeStruct)
    return pl.pallas_call(
        kernel,
        out_shape=out_shape,
        in_specs=[vmem] * len(operands),
        out_specs=vmem if single else [vmem] * len(out_shape),
        compiler_params=pltpu.CompilerParams(vmem_limit_bytes=16 * 2**20),
        cost_estimate=pl.CostEstimate(
            flops=flops, bytes_accessed=sum(x.size * 2 for x in operands), transcendentals=0
        ),
    )(*operands)


def local(embeddings, assignment):
    home = ("yl", "x", "core")
    far_y = lax.axis_size("yh")
    n = lax.axis_size("z")
    places = len(PLACES)
    owners = far_y * places
    width = embeddings.shape[1]
    per_owner = 2 * embeddings.shape[0] // owners
    slots = owners * per_owner
    rows = embeddings.shape[0]
    send = on_chip(
        send_kernel,
        jax.ShapeDtypeStruct((slots, width), jnp.bfloat16),
        2 * slots * rows * width,
        embeddings,
        assignment.reshape(1, rows),
    )
    own = lax.all_to_all(
        send.reshape(owners, per_owner, width),
        ("yh", "z"),
        split_axis=0,
        concat_axis=0,
        tiled=True,
    ).reshape(slots, width)
    tile = 2 * slots * slots * width
    x1 = from_place(own, X1)
    y = from_place(own, Y)
    x2 = from_place(x1, X1)
    stats = jax.ShapeDtypeStruct((ROWS, slots), jnp.float32)
    near = on_chip(near_kernel, stats, 6 * tile, own, y, x1)
    first, later, near = lax.optimization_barrier((own, y, near))
    c = from_place(first, C)
    yc = from_place(later, C)
    seen = on_chip(far_kernel, stats, 2 * tile, near, own, y, x2)
    message = on_chip(
        last_kernel,
        jax.ShapeDtypeStruct((n * ROWS // GROUP, GROUP * CELLS), jnp.float32),
        8 * tile,
        seen,
        own,
        y,
        c,
        yc,
        x1,
        x2,
    )
    message = message.reshape(n, ROWS // GROUP, GROUP * CELLS)
    message = lax.all_to_all(message, home, split_axis=0, concat_axis=0, tiled=True)
    found = on_chip(
        finish_kernel,
        jax.ShapeDtypeStruct((2, slots), jnp.float32),
        0,
        message.reshape(places * ROWS // GROUP, GROUP * CELLS),
    )
    pairs = [(u * n + z, z * n + u) for u in range(places) for z in range(n)]
    found = lax.ppermute(found, home + ("z",), pairs)
    return found[0].reshape(1, 1, slots), found[1].reshape(1, 1, slots)


def solution(mesh):
    names = ("yh", "yl", "x", "core", "z")
    n = mesh.shape["split"]
    parts = Mesh(mesh.devices.reshape(-1, *HOME, n), names)
    in_specs = (P(names, None), P(names))
    out_specs = (P(names[:4], "z", None), P(names[:4], "z", None))
    return jax.shard_map(local, mesh=parts, in_specs=in_specs, out_specs=out_specs, check_vma=False)
```

```python
import itertools

import jax
import jax.numpy as jnp
from jax import lax
from jax.experimental import pallas as pl
from jax.experimental.pallas import tpu as pltpu
from jax.sharding import Mesh
from jax.sharding import PartitionSpec as P

EPSILON = 1e-06
NEVER = -2.0
DEAD_MARK = 2.0


DEAD_BEST = -8.0
ROWS = 16
HOME = (2, 4, 2)
OWN, C, Y, YC = (0, 0, 0), (0, 0, 1), (1, 0, 0), (1, 0, 1)
X1, X2 = (0, 3, 0), (0, 2, 0)
TARGETS = (OWN, C, Y, YC, X1)
COUNT = len(TARGETS)


def plus(a, b):
    return tuple((x + y) % d for x, y, d in zip(a, b, HOME))


def number(place):
    return (place[0] * HOME[1] + place[1]) * HOME[2] + place[2]


PLACES = list(itertools.product(*[range(d) for d in HOME]))


def from_place(value, d):
    pairs = [(number(plus(u, d)), number(u)) for u in PLACES]
    return lax.ppermute(value, ("yl", "x", "core"), pairs)


def dots(a, b):
    return lax.dot_general(a, b, (((1,), (1,)), ((), ())), preferred_element_type=jnp.float32)


def best_and_sum(far, rows, diagonal=False):
    alive = far[:, 0:1].astype(jnp.float32) < 1.5
    scores = dots(far, rows)
    total = jnp.sum(jnp.where(alive, scores, 0.0), axis=0, keepdims=True)
    if diagonal:
        same = lax.broadcasted_iota(jnp.int32, scores.shape, 0) == lax.broadcasted_iota(
            jnp.int32, scores.shape, 1
        )
        scores = jnp.where(same, NEVER, scores)
    return jnp.max(jnp.where(alive, scores, NEVER), axis=0, keepdims=True), total


def send_kernel(embeddings, assignment, out):
    values = embeddings[...].astype(jnp.float32)
    scale = lax.rsqrt(jnp.sum(values * values, axis=1, keepdims=True) + EPSILON)
    normed = (values * scale).astype(jnp.bfloat16)
    rows, slots = values.shape[0], out.shape[0]
    along = jnp.broadcast_to(assignment[...].astype(jnp.float32), (rows, rows))
    earlier = iota((rows, rows), 0) < iota((rows, rows), 1)
    rank = jnp.sum(jnp.where((along == along.T) & earlier, 1.0, 0.0), axis=0, keepdims=True)
    slot = along[0:1] * (slots // 64) + rank
    table = (slot == iota((slots, rows), 0).astype(jnp.float32)).astype(jnp.float32)
    placed = jnp.dot(table.astype(jnp.bfloat16), normed, preferred_element_type=jnp.float32)
    empty = jnp.sum(table, axis=1, keepdims=True) < 0.5
    mark = empty & (iota(placed.shape, 1) == 0)
    out[...] = jnp.where(mark, DEAD_MARK, placed).astype(jnp.bfloat16)


def merge(old, new):
    return (jnp.maximum(old[0], new[0]), old[1] + new[1])


def near_kernel(own, y, x1, out):
    a, b, d = own[...], y[...], x1[...]
    stats = [
        merge(merge(best_and_sum(a, a, True), best_and_sum(b, a)), best_and_sum(d, a)),
        best_and_sum(d, b),
        merge(best_and_sum(a, d), best_and_sum(b, d)),
    ]
    first = (iota((8, own.shape[1]), 1) == 0).astype(jnp.bfloat16)
    marks = [dots(first, x)[0:1] for x in (a, b, d)]
    out[...] = jnp.concatenate(
        [b for b, _ in stats] + [t for _, t in stats] + marks + marks[0:1] * (ROWS - 9)
    )


def far_kernel(near, own, y, x2, out):
    far = x2[...]
    a, b = best_and_sum(far, own[...]), best_and_sum(far, y[...])
    best = jnp.maximum(near[0:2, :], jnp.concatenate([a[0], b[0]]))
    total = near[3:5, :] + jnp.concatenate([a[1], b[1]])
    out[...] = jnp.concatenate([best, near[2:3, :], total, near[5:ROWS, :]])


def iota(shape, axis):
    return lax.broadcasted_iota(jnp.int32, shape, axis)


def exact_dot(a, b):
    return lax.dot_general(
        a,
        b,
        (((1,), (0,)), ((), ())),
        precision=lax.Precision.HIGHEST,
        preferred_element_type=jnp.float32,
    )


GROUP = 8
CELLS = 16


def cell_of(slot):
    return slot // 64 * 4 + slot % 4


def place_of(slot):
    return slot // 4 % 16


def last_kernel(seen, own, y, c, yc, x1, x2, out):
    held = [own[...], c[...], y[...], yc[...], x1[...]]
    far = x2[...]
    stats = [
        merge(best_and_sum(held[1], held[0]), best_and_sum(held[3], held[0])),
        merge(best_and_sum(held[4], held[1]), best_and_sum(far, held[1])),
        (seen[1:2, :], seen[4:5, :]),
        merge(best_and_sum(held[4], held[3]), best_and_sum(far, held[3])),
        merge(best_and_sum(held[1], held[4]), best_and_sum(held[3], held[4])),
    ]
    stats[0] = merge(stats[0], (seen[0:1, :], seen[3:4, :]))
    stats[4] = merge(stats[4], (seen[2:3, :], seen[5:6, :]))
    best = jnp.concatenate([b for b, _ in stats])
    total = jnp.concatenate([t for _, t in stats])
    slots = best.shape[1]
    first = (iota((8, own.shape[1]), 1) == 0).astype(jnp.bfloat16)
    marks = [dots(first, x)[0:1] for x in (held[1], held[3])]
    alive = (
        jnp.concatenate([seen[6:7, :], marks[0], seen[7:8, :], marks[1], seen[8:9, :]]) < 1.5
    )
    square = jnp.sum(jnp.where(alive, total, 0.0))
    best = jnp.concatenate([jnp.where(alive[0:1], best[0:1], DEAD_BEST), best[1:]], axis=0)
    values = jnp.concatenate(
        [best, total, jnp.full((ROWS - 2 * COUNT, slots), square, jnp.float32)], axis=0
    )
    n = out.shape[0] * GROUP // ROWS
    shape = (n, ROWS, slots)
    chosen = jnp.where(place_of(iota(shape, 2)) == iota(shape, 0), values[None], 0.0)
    shape = (slots, GROUP * CELLS)
    spread = (cell_of(iota(shape, 0)) == iota(shape, 1) % CELLS).astype(jnp.float32)
    wide = exact_dot(chosen.reshape(n * ROWS, slots), spread).reshape(-1, GROUP, GROUP * CELLS)
    keep = iota(wide.shape, 2) // CELLS == iota(wide.shape, 1)
    out[...] = jnp.sum(jnp.where(keep, wide, 0.0), axis=1)


def finish_kernel(arrived, out):
    slots = out.shape[1]
    places = arrived.shape[0] * GROUP // ROWS
    shape = (arrived.shape[0], GROUP, GROUP * CELLS)
    keep = iota(shape, 2) // CELLS == iota(shape, 1)
    rows = jnp.where(keep, arrived[...][:, None, :], 0.0).reshape(places * ROWS, GROUP * CELLS)
    shape = (GROUP * CELLS, slots)
    spread = (cell_of(iota(shape, 1)) == iota(shape, 0) % CELLS).astype(jnp.float32)
    wide = exact_dot(rows, spread).reshape(places, ROWS, slots)
    u, v, to = (iota(wide.shape, axis) for axis in range(3))
    target = v % COUNT
    core = (u ^ jnp.where((target == 1) | (target == 3), 1, 0)) & 1
    low = (u ^ jnp.where((target == 2) | (target == 3), 8, 0)) & 8
    across = (u + jnp.where(target == 4, 6, 0)) & 6
    here = (core + low + across == place_of(to)) | (v >= 2 * COUNT)
    result = jnp.sum(jnp.where(here, wide, 0.0), axis=0)
    alive = result[0:1] > NEVER - 1.0
    best = jnp.max(result[0:COUNT], axis=0, keepdims=True)
    nearest = jnp.where(alive, best, 0.0)
    square = jnp.maximum(result[2 * COUNT : 2 * COUNT + 1], 0.0)
    total = jnp.sum(result[COUNT : 2 * COUNT], axis=0, keepdims=True)
    cosine = total * lax.rsqrt(square + EPSILON)
    distance = jnp.where(alive, 1.0 - cosine, 0.0)
    out[...] = jnp.concatenate([nearest, distance])


def on_chip(kernel, out_shape, flops, *operands):
    vmem = pl.BlockSpec(memory_space=pltpu.VMEM)
    single = isinstance(out_shape, jax.ShapeDtypeStruct)
    return pl.pallas_call(
        kernel,
        out_shape=out_shape,
        in_specs=[vmem] * len(operands),
        out_specs=vmem if single else [vmem] * len(out_shape),
        compiler_params=pltpu.CompilerParams(vmem_limit_bytes=16 * 2**20),
        cost_estimate=pl.CostEstimate(
            flops=flops, bytes_accessed=sum(x.size * 2 for x in operands), transcendentals=0
        ),
    )(*operands)


def local(embeddings, assignment):
    home = ("yl", "x", "core")
    far_y = lax.axis_size("yh")
    n = lax.axis_size("z")
    places = len(PLACES)
    owners = far_y * places
    width = embeddings.shape[1]
    per_owner = 2 * embeddings.shape[0] // owners
    slots = owners * per_owner
    rows = embeddings.shape[0]
    send = on_chip(
        send_kernel,
        jax.ShapeDtypeStruct((slots, width), jnp.bfloat16),
        2 * slots * rows * width,
        embeddings,
        assignment.reshape(1, rows),
    )
    own = lax.all_to_all(
        send.reshape(owners, per_owner, width),
        ("yh", "z"),
        split_axis=0,
        concat_axis=0,
        tiled=True,
    ).reshape(slots, width)
    tile = 2 * slots * slots * width
    x1 = from_place(own, X1)
    y = from_place(own, Y)
    x2 = from_place(x1, X1)
    stats = jax.ShapeDtypeStruct((ROWS, slots), jnp.float32)
    near = on_chip(near_kernel, stats, 6 * tile, own, y, x1)
    first, later, near = lax.optimization_barrier((own, y, near))
    c = from_place(first, C)
    yc = from_place(later, C)
    seen = on_chip(far_kernel, stats, 2 * tile, near, own, y, x2)
    message = on_chip(
        last_kernel,
        jax.ShapeDtypeStruct((n * ROWS // GROUP, GROUP * CELLS), jnp.float32),
        8 * tile,
        seen,
        own,
        y,
        c,
        yc,
        x1,
        x2,
    )
    message = message.reshape(n, ROWS // GROUP, GROUP * CELLS)
    message = lax.all_to_all(message, home, split_axis=0, concat_axis=0, tiled=True)
    found = on_chip(
        finish_kernel,
        jax.ShapeDtypeStruct((2, slots), jnp.float32),
        0,
        message.reshape(places * ROWS // GROUP, GROUP * CELLS),
    )
    pairs = [(u * n + z, z * n + u) for u in range(places) for z in range(n)]
    found = lax.ppermute(found, home + ("z",), pairs)
    return found[0].reshape(1, 1, slots), found[1].reshape(1, 1, slots)


def solution(mesh):
    names = ("yh", "yl", "x", "core", "z")
    n = mesh.shape["split"]
    parts = Mesh(mesh.devices.reshape(-1, *HOME, n), names)
    in_specs = (P(names, None), P(names))
    out_specs = (P(names[:4], "z", None), P(names[:4], "z", None))
    return jax.shard_map(local, mesh=parts, in_specs=in_specs, out_specs=out_specs, check_vma=False)
```
